32 devices in a mesh: dp: 8 (over z, x), seq: 4 (over y, core).
Axes of the slice: x: 2, y: 2, z: 4, core: 2. Of those that a mesh axis runs over, the one named last changes fastest.
Arguments:
- enc_rows: bfloat16 [32, 256, 1280], P('dp', 'seq'), may hold values from -100 to 100
- out_weight: bfloat16 [1280, 512], replicated, may hold values from -3 to 3
- labels: int32 [32, 63], P('dp'), may hold values from 1 to 511
- label_count: int32 [32], P('dp'), may hold values from 1 to 63, as said below
- frame_count: int32 [32], P('dp'), may hold values from 128 to 256, as said below
Outputs:
- logit_grad: bfloat16 [32, 256, 512], P('dp', 'seq')
- row_grad: bfloat16 [32, 256, 1280], P('dp', 'seq')
- weight_grad: float32 [1280, 512], P('dp', 'seq')
The draws below stay inside these ranges and needn't reach their ends.
Inputs may be any that keep to these rules, and one draw needn't show every extreme that they name: `labels`: character ids; id 0 is the blank and never appears. `label_count`: some utterance has 63 labels in every draw. `frame_count`: some utterance has 256 frames in every draw.
All inputs are finite; a program needn't handle non-finite values.
Results may differ from the reference program's by a relative error of at most 0.0043.
Values sent between devices are 32-bit elements; how exact they have to be, the bound alone decides.
A program may use at most 64 MiB of HBM per device.

```python
import math
import jax
import jax.numpy as jnp
from jax import lax

D = 1280
V = 512
SEQS = 4
FRAMES = 256
L = 63
BATCH = 32
N_DP = 8


def weight_table(key):
    spread = 3.0 / math.sqrt(D)
    drawn = jax.random.normal(jax.random.fold_in(key, 11), (D, V), jnp.float32) * spread
    return jnp.clip(drawn, -3.0, 3.0)


def draw_out_weight(key, part):
    return weight_table(key).astype(jnp.bfloat16)


def draw_enc_rows(key, part):
    base_rows = jnp.clip(jax.random.normal(jax.random.fold_in(key, 21), (BATCH, FRAMES, D), jnp.float32), -6.0, 6.0)
    return jnp.clip(base_rows, -100.0, 100.0).astype(jnp.bfloat16)


def forced_most(key, lowest, highest):
    drawn = jax.random.randint(jax.random.fold_in(key, 31), (BATCH,), lowest, highest + 1)
    forced_spot = jax.random.randint(jax.random.fold_in(key, 32), (), 0, BATCH)
    return jnp.where(jnp.arange(BATCH) == forced_spot, highest, drawn).astype(jnp.int32)


def draw_frame_count(key, part):
    return forced_most(jax.random.fold_in(key, 51), FRAMES // 2, FRAMES)


def draw_label_count(key, part):
    return forced_most(jax.random.fold_in(key, 41), 1, L)


def place_ends(values, own_key, smallest, top_value):
    longest = values.shape.index(max(values.shape))
    spots = []
    for shift in (0, 1):
        where = [jax.random.randint(jax.random.fold_in(own_key, axis), (), 0, length) for axis, length in enumerate(values.shape)]
        where[longest] = (where[longest] + shift) % values.shape[longest]
        spots.append(tuple(where))
    return values.at[spots[0]].set(smallest).at[spots[1]].set(top_value)


def setup_inputs(seed: int = 0) -> dict:
    streams_of = jax.random.split(jax.random.key(seed), 6)
    return {
        "enc_rows": draw_enc_rows(jax.random.fold_in(streams_of[5], 71), 0),
        "out_weight": draw_out_weight(jax.random.fold_in(streams_of[5], 71), 0),
        "labels": place_ends(jax.random.randint(streams_of[2], (BATCH, L), 1, V), jax.random.fold_in(streams_of[2], 1), 1, V - 1).astype(jnp.int32),
        "label_count": draw_label_count(jax.random.fold_in(streams_of[5], 71), 0),
        "frame_count": draw_frame_count(jax.random.fold_in(streams_of[5], 71), 0),
    }


negative_fill = -1.0e30


def merge_three(first_term, second_term, third_term):
    highest = jnp.maximum(jnp.maximum(first_term, second_term), third_term)
    return highest + jnp.log(jnp.exp(first_term - highest) + jnp.exp(second_term - highest) + jnp.exp(third_term - highest))


def shift_right(values, amount):
    filler = jnp.full((values.shape[0], amount), negative_fill, jnp.float32)
    return jnp.concatenate([filler, values[:, :-amount]], axis=1)


def shift_left(values, amount):
    filler = jnp.full((values.shape[0], amount), negative_fill, jnp.float32)
    return jnp.concatenate([values[:, amount:], filler], axis=1)


def advance(current, emission, usable, allowed):
    from_one = shift_right(current, 1)
    from_two = jnp.where(allowed, shift_right(current, 2), negative_fill)
    fresh = merge_three(current, from_one, from_two) + emission
    return jnp.where(usable[:, None], fresh, current)


def retreat(current, emission, usable, allowed_next):
    summed = current + emission
    next_one = shift_left(summed, 1)
    next_two = jnp.where(allowed_next, shift_left(summed, 2), negative_fill)
    fresh = merge_three(summed, next_one, next_two)
    return jnp.where(usable[:, None], fresh, current)


def lattice(labels, label_count):
    utterances, length = labels.shape
    states_wide = 2 * length + 2
    blanks = jnp.zeros((utterances, length + 1), jnp.int32)
    chars = jnp.concatenate([labels, jnp.full((utterances, 1), -1, jnp.int32)], axis=1)
    extended = jnp.stack([blanks, chars], axis=2).reshape(utterances, states_wide)
    earlier = jnp.concatenate([jnp.full((utterances, 2), -2, jnp.int32), extended[:, :-2]], axis=1)
    positions = jnp.arange(states_wide, dtype=jnp.int32)[None, :]
    allowed = (positions % 2 == 1) & (positions >= 3) & (extended != earlier)
    allowed_next = jnp.concatenate([allowed[:, 2:], jnp.zeros((utterances, 2), jnp.bool_)], axis=1)
    zeros_row = jnp.zeros((utterances, states_wide), jnp.float32)
    initial = jnp.where(positions == 0, zeros_row, negative_fill)
    doubled = 2 * label_count[:, None]
    closing = jnp.where((positions == doubled) | (positions == doubled - 1), zeros_row, negative_fill)
    return allowed, allowed_next, initial, closing


def emissions(logprob, labels):
    utterances, frames, vocabulary = logprob.shape
    length = labels.shape[1]
    char_index = jnp.concatenate([jnp.zeros((utterances, 1), jnp.int32), labels], axis=1)
    picked = jnp.take_along_axis(logprob, jnp.broadcast_to(char_index[:, None, :], (utterances, frames, length + 1)), axis=2)
    blank_part = jnp.broadcast_to(picked[:, :, :1], picked.shape)
    label_part = jnp.concatenate([picked[:, :, 1:], jnp.full((utterances, frames, 1), negative_fill, jnp.float32)], axis=2)
    emission = jnp.stack([blank_part, label_part], axis=3).reshape(utterances, frames, 2 * length + 2)
    return jnp.swapaxes(emission, 0, 1), char_index


def forward_pass(initial, emission, usable, allowed):
    def frame_step(current, inputs):
        fresh = advance(current, inputs[0], inputs[1], allowed)
        return fresh, fresh
    return lax.scan(frame_step, initial, (emission, usable))


def backward_pass(closing, emission, usable, allowed_next):
    def frame_step(current, inputs):
        return retreat(current, inputs[0], inputs[1], allowed_next), current
    return lax.scan(frame_step, closing, (emission, usable), reverse=True)


def gradients(logprob, forward_states, backward_states, usable, char_index):
    frames, utterances, states_wide = forward_states.shape
    summed = forward_states + backward_states
    highest = jnp.max(summed, axis=2, keepdims=True)
    log_total = highest + jnp.log(jnp.sum(jnp.exp(summed - highest), axis=2, keepdims=True))
    posterior = jnp.exp(summed - log_total) * usable[:, :, None].astype(jnp.float32)
    paired = posterior.reshape(frames, utterances, states_wide // 2, 2)
    blank_mass = jnp.sum(paired[:, :, :, 0], axis=2, keepdims=True)
    occupancy = jnp.concatenate([blank_mass, paired[:, :, :-1, 1]], axis=2)
    vocabulary = logprob.shape[2]
    one_hot = (char_index[:, :, None] == jnp.arange(vocabulary, dtype=jnp.int32)[None, None, :]).astype(jnp.float32)
    char_mass = jnp.einsum("fup,upv->ufv", occupancy, one_hot, precision=lax.Precision.HIGHEST)
    keep = jnp.swapaxes(usable, 0, 1)[:, :, None].astype(jnp.float32)
    return ((jnp.exp(logprob) - char_mass) * keep).astype(jnp.bfloat16)


def reference(enc_rows, out_weight, labels, label_count, frame_count):
    def one_block(inputs):
        block_rows, block_labels, block_lcount, block_fcount = inputs
        utterances, frames, width_rows = block_rows.shape
        flat_rows = block_rows.reshape(utterances * frames, width_rows)
        logits = jnp.dot(flat_rows, out_weight, preferred_element_type=jnp.float32).reshape(utterances, frames, -1)
        logprob = jax.nn.log_softmax(logits, axis=-1)
        emission, char_index = emissions(logprob, block_labels)
        allowed, allowed_next, initial, closing = lattice(block_labels, block_lcount)
        usable = jnp.arange(frames, dtype=jnp.int32)[:, None] < block_fcount[None, :]
        forward_states = forward_pass(initial, emission, usable, allowed)[1]
        backward_states = backward_pass(closing, emission, usable, allowed_next)[1]
        logit_grad = gradients(logprob, forward_states, backward_states, usable, char_index)
        flat_grad = logit_grad.reshape(utterances * frames, -1)
        row_grad = lax.dot_general(flat_grad, out_weight, (((1,), (1,)), ((), ())), preferred_element_type=jnp.float32)
        row_grad = row_grad.astype(jnp.bfloat16).reshape(utterances, frames, width_rows)
        weight_term = lax.dot_general(flat_rows, flat_grad, (((0,), (0,)), ((), ())), preferred_element_type=jnp.float32)
        return logit_grad, row_grad, weight_term

    blocks = (enc_rows.reshape(N_DP, SEQS, FRAMES, D), labels.reshape(N_DP, SEQS, L),
              label_count.reshape(N_DP, SEQS), frame_count.reshape(N_DP, SEQS))
    logit_grad, row_grad, weight_terms = lax.map(one_block, blocks)
    weight_grad = jnp.sum(weight_terms, axis=0) / BATCH
    return logit_grad.reshape(BATCH, FRAMES, V), row_grad.reshape(BATCH, FRAMES, D), weight_grad
```

```python
import functools

import jax
import jax.numpy as jnp
from jax import lax
from jax.experimental import pallas as pl
from jax.experimental.pallas import tpu as pltpu
from jax.sharding import PartitionSpec as P

negative_fill = -1e30
LOG2_E = 1.4426950408889634
LANES = 128
SUBLANES = 8
SPLIT = 2
UNROLL = 32
MESH = pl.DeviceIdType.MESH
BOTH_LAST = (((1,), (1,)), ((), ()))


def three_parts(values):
    high = values.astype(jnp.bfloat16)
    rest = values - high.astype(jnp.float32)
    middle = rest.astype(jnp.bfloat16)
    low = (rest - middle.astype(jnp.float32)).astype(jnp.bfloat16)
    return high, middle, low


def label_table(labels_ref, table_ref):
    utterances, length = labels_ref.shape
    table_ref[...] = jnp.zeros_like(table_ref)
    table_ref[0:utterances, 0:length] = labels_ref[...]
    table_ref[utterances:2 * utterances, 0:length] = labels_ref[...]
    return table_ref[...]


def take_lanes(values, index):
    return jnp.take_along_axis(values, index, axis=1)


def character_tables(labels_ref, table_ref, hot_ref):
    groups, _, vocabulary = hot_ref.shape
    utterances, length = labels_ref.shape
    slots = length + 1
    pack = utterances // groups
    width = slots // SPLIT
    table = label_table(labels_ref, table_ref)
    lane = lax.broadcasted_iota(jnp.int32, table.shape, 1)
    within = lax.rem(lane, slots)
    order = lax.rem(within, width) * SPLIT + within // width
    chars = take_lanes(table, order).astype(jnp.float32)
    row_lane = lax.broadcasted_iota(jnp.int32, (1, LANES), 1)
    columns = lax.broadcasted_iota(jnp.int32, (LANES, LANES), 1).astype(jnp.float32)
    for group in range(groups):
        first = group * pack
        line = chars[first:first + 1, :]
        for inner in range(1, pack):
            line = jnp.where(row_lane >= inner * slots, chars[first + inner:first + inner + 1, :], line)
        down = jnp.transpose(jnp.broadcast_to(line, (LANES, LANES)))
        for low in range(0, vocabulary, LANES):
            hot_ref[group, :, low:low + LANES] = jnp.where(
                down == columns + float(low), 1.0, 0.0
            ).astype(jnp.bfloat16)


def share_emissions(seq_count, enc_ref, weight_ref, labels_ref, prob_ref, gathered_ref, hot_ref,
                    table_ref, send_sems, recv_sems, before_sending, meanwhile):
    utterances, length = labels_ref.shape
    me = lax.axis_index("seq")
    frames = enc_ref.shape[0] // utterances
    groups = gathered_ref.shape[0]
    pack = utterances // groups
    slots = length + 1
    own = pl.ds(pl.multiple_of(me * frames, frames), frames)
    character_tables(labels_ref, table_ref, hot_ref)
    logits = jnp.dot(enc_ref[...], weight_ref[...], preferred_element_type=jnp.float32)
    highest = jnp.max(logits, axis=1, keepdims=True)
    shifted = logits - highest
    powers = jnp.exp(shifted)
    total = jnp.sum(powers, axis=1, keepdims=True)
    logprob = shifted - jnp.log(total)
    prob_ref[...] = powers * (1.0 / total)
    lane = lax.broadcasted_iota(jnp.int32, (frames, LANES), 1)
    for group in range(groups):
        rows = pack * frames
        mine = logprob[group * rows:(group + 1) * rows]
        picked = None
        for part in three_parts(mine):
            product = lax.dot_general(part, hot_ref[group], BOTH_LAST, preferred_element_type=jnp.float32)
            picked = product if picked is None else picked + product
        packed = picked[:frames]
        for inner in range(1, pack):
            packed = jnp.where(lane >= inner * slots, picked[inner * frames:(inner + 1) * frames], packed)
        gathered_ref[group, own, :] = packed * LOG2_E
    before_sending()
    copies = []
    for step in range(1, seq_count):
        peer = lax.rem(me + step, seq_count)
        copy = pltpu.make_async_remote_copy(
            src_ref=gathered_ref.at[:, own],
            dst_ref=gathered_ref.at[:, own],
            send_sem=send_sems.at[step - 1],
            recv_sem=recv_sems.at[step - 1],
            device_id={"seq": peer},
            device_id_type=MESH,
        )
        copy.start()
        copies.append(copy)
    meanwhile()
    for copy in copies:
        copy.wait()


def spread(count_ref, utterance):
    values = jnp.full(utterance.shape, count_ref[0], jnp.int32)
    for u in range(1, count_ref.shape[0]):
        values = jnp.where(utterance == u, count_ref[u], values)
    return values


def lattice_gradients(label_count_ref, frame_count_ref, gathered_ref, labels_ref, prob_ref, hot_ref,
                      logit_ref, table_ref, ahead_ref, back_ref, mass_ref):
    utterances, length = labels_ref.shape
    groups, steps = gathered_ref.shape[:2]
    frames = prob_ref.shape[0] // utterances
    rows = 2 * utterances
    slots = length + 1
    width = slots // SPLIT
    pack = utterances // groups
    span = LANES * SPLIT
    shape = (rows, LANES)
    row = lax.broadcasted_iota(jnp.int32, shape, 0)
    lane = lax.broadcasted_iota(jnp.int32, shape, 1)
    forward = row < utterances
    utterance = lax.rem(row, utterances)
    offset = lax.rem(utterance, pack) * slots
    label_rows = table_ref[...]
    label_count = spread(label_count_ref, utterance)
    frame_count = spread(frame_count_ref, utterance)
    first_usable = jnp.where(forward, 0, steps - frame_count)

    label_fill, jump_fill, label_start, blank_start = [], [], [], []
    for r in range(SPLIT):
        run = jnp.where(forward, r, SPLIT - 1 - r)
        j = lane * SPLIT + run
        real = j < length
        label_fill.append(jnp.where(real, 0.0, negative_fill))
        before = jnp.where(forward, j - 1, j + 1)
        here_char = take_lanes(label_rows, jnp.clip(j, 0, LANES - 1))
        before_char = take_lanes(label_rows, jnp.clip(before, 0, LANES - 1))
        can_jump = real & (before >= 0) & (before < length) & (here_char != before_char)
        jump_fill.append(jnp.where(can_jump, 0.0, negative_fill))
        label_begin = j == jnp.where(forward, 0, label_count - 1)
        label_start.append(jnp.where(label_begin, 0.0, negative_fill))
        blank = jnp.where(forward, j, lax.rem(j + 1, span))
        blank_begin = blank == jnp.where(forward, 0, label_count)
        blank_start.append(jnp.where(blank_begin, 0.0, negative_fill))
    blank_index = offset + slots - 1
    inner_of = lax.rem(utterance, pack)
    row_group = utterance // pack

    def frame_row(group, step):
        return jnp.broadcast_to(gathered_ref[group, pl.ds(step, 1), :], shape)

    def raw_emission(step):
        raw = None
        for group in range(groups):
            early = frame_row(group, step)
            late = frame_row(group, steps - 1 - step)
            both = jnp.where(forward, early, late)
            raw = both if raw is None else jnp.where(row_group == group, both, raw)
        return raw

    def label_emissions(raw):
        turned = {}
        for begin in range(0, pack * slots, width):
            turned[begin] = pltpu.roll(raw, LANES - begin, 1) if begin else raw
        found = []
        for r in range(SPLIT):
            chosen = None
            for inner in range(pack):
                ahead = turned[inner * slots + r * width]
                back = turned[inner * slots + (SPLIT - 1 - r) * width]
                both = jnp.where(forward, ahead, back)
                chosen = both if chosen is None else jnp.where(inner_of == inner, both, chosen)
            found.append(chosen + label_fill[r])
        return found

    def behind(values):
        return jnp.where(forward, pltpu.roll(values, 1, 1), pltpu.roll(values, LANES - 1, 1))

    def one_step(step, state, resets):
        labels_v, blanks_v, labels_x, blanks_x = state
        raw = raw_emission(step)
        blank_emission = take_lanes(raw, blank_index)
        label_emission = label_emissions(raw)
        ahead_row = pl.ds(pl.multiple_of(step * rows, rows), rows)
        back_row = pl.ds(pl.multiple_of((steps - 1 - step) * rows, rows), rows)
        full_labels, full_blanks = [], []
        for r in range(SPLIT):
            full_labels.append(labels_v[r] + label_emission[r])
            full_blanks.append(blanks_v[r] + blank_emission)
            ahead_ref[r, ahead_row, :] = full_labels[r]
            ahead_ref[SPLIT + r, ahead_row, :] = full_blanks[r]
            ahead_ref[2 * SPLIT + r, ahead_row, :] = labels_x[r]
            ahead_ref[3 * SPLIT + r, ahead_row, :] = blanks_x[r]
            back_ref[r, back_row, :] = labels_v[r]
            back_ref[SPLIT + r, back_row, :] = blanks_v[r]
            back_ref[2 * SPLIT + r, back_row, :] = labels_x[r]
            back_ref[3 * SPLIT + r, back_row, :] = blanks_x[r]
        if resets:
            usable = step >= first_usable
        next_labels_v, next_blanks_v, next_labels_x, next_blanks_x = [], [], [], []
        for r in range(SPLIT):
            if r == 0:
                behind_v = behind(full_labels[SPLIT - 1])
                behind_x = behind(labels_x[SPLIT - 1])
            else:
                behind_v = full_labels[r - 1]
                behind_x = labels_x[r - 1]
            jump_v = behind_v + jump_fill[r]
            pivot = jnp.maximum(jnp.maximum(full_blanks[r], full_labels[r]), jump_v)
            fresh_x = (
                jnp.exp2(full_labels[r] - pivot) * labels_x[r]
                + jnp.exp2(full_blanks[r] - pivot) * blanks_x[r]
                + jnp.exp2(jump_v - pivot) * behind_x
            )
            if resets:
                pivot = jnp.where(usable, pivot, label_start[r])
                fresh_x = jnp.where(usable, fresh_x, 1.0)
            next_labels_v.append(pivot)
            next_labels_x.append(fresh_x)
            pivot = jnp.maximum(full_blanks[r], behind_v)
            fresh_x = (
                jnp.exp2(full_blanks[r] - pivot) * blanks_x[r]
                + jnp.exp2(behind_v - pivot) * behind_x
            )
            if resets:
                pivot = jnp.where(usable, pivot, blank_start[r])
                fresh_x = jnp.where(usable, fresh_x, 1.0)
            next_blanks_v.append(pivot)
            next_blanks_x.append(fresh_x)
        return (tuple(next_labels_v), tuple(next_blanks_v), tuple(next_labels_x), tuple(next_blanks_x))

    ones = (jnp.ones(shape, jnp.float32),) * SPLIT

    def run_block(resets, block, state):
        labels_v, blanks_v = state
        full = (labels_v, blanks_v, ones, ones)
        for inner in range(UNROLL):
            full = one_step(block * UNROLL + inner, full, resets)
        labels_v, blanks_v, labels_x, blanks_x = full
        labels_v = tuple(v + jnp.log2(x) for v, x in zip(labels_v, labels_x))
        blanks_v = tuple(v + jnp.log2(x) for v, x in zip(blanks_v, blanks_x))
        return labels_v, blanks_v

    blocks = steps // UNROLL
    resetting = (steps // 2) // UNROLL
    state = (tuple(label_start), tuple(blank_start))
    state = lax.fori_loop(0, resetting, functools.partial(run_block, True), state)
    lax.fori_loop(resetting, blocks, functools.partial(run_block, False), state)

    start = lax.axis_index("seq") * frames
    inner_frame = row // utterances

    def posterior_block(block, carry):
        for pair in range(0, SUBLANES, 2):
            low = block * SUBLANES + pair
            first = pl.multiple_of((start + low) * rows, rows)

            def ahead(index):
                return jnp.where(
                    forward, ahead_ref[index, pl.ds(first, rows), :],
                    ahead_ref[index, pl.ds(first + utterances, rows), :],
                )

            def back(index):
                return jnp.where(
                    forward, back_ref[index, pl.ds(first + utterances, rows), :],
                    back_ref[index, pl.ds(first + rows, rows), :],
                )

            def term(ahead_index, back_index, turn):
                level, factor = back(back_index), back(2 * SPLIT + back_index)
                if turn:
                    level, factor = pltpu.roll(level, 1, 1), pltpu.roll(factor, 1, 1)
                factor = factor * ahead(2 * SPLIT + ahead_index)
                return (ahead(ahead_index) + level) + jnp.log2(factor)

            terms = [term(r, SPLIT - 1 - r, False) for r in range(SPLIT)]
            terms += [term(SPLIT + r, SPLIT + (SPLIT - r) % SPLIT, r == 0) for r in range(SPLIT)]
            highest = jnp.max(functools.reduce(jnp.maximum, terms), axis=1, keepdims=True)
            powers = [jnp.exp2(value - highest) for value in terms]
            blank_mass = jnp.sum(functools.reduce(jnp.add, powers[SPLIT:]), axis=1, keepdims=True)
            total = blank_mass + jnp.sum(functools.reduce(jnp.add, powers[:SPLIT]), axis=1, keepdims=True)
            usable = start + low + inner_frame < frame_count
            scale = jnp.where(usable, 1.0 / total, 0.0)
            mass = jnp.where(lane == offset + slots - 1, blank_mass, 0.0)
            for inner in range(pack):
                spread_out = None
                for r in range(SPLIT):
                    shift = inner * slots + r * width
                    moved = pltpu.roll(powers[r], shift, 1) if shift else powers[r]
                    spread_out = moved if spread_out is None else spread_out + moved
                mass += spread_out if pack == 1 else jnp.where(inner_of == inner, spread_out, 0.0)
            mass_ref[pl.ds(pl.multiple_of(low * utterances, rows), rows), :] = mass * scale
        return carry

    lax.fori_loop(0, frames // SUBLANES, posterior_block, 0)

    times = start + lax.broadcasted_iota(jnp.int32, (frames, 1), 0)
    for u in range(utterances):
        own = slice(u * frames, (u + 1) * frames)
        hot = hot_ref[u // pack]
        mass = None
        for part in three_parts(mass_ref[pl.ds(u, frames, stride=utterances), :])[:2]:
            product = jnp.dot(part, hot, preferred_element_type=jnp.float32)
            mass = product if mass is None else mass + product
        kept = jnp.where(times < frame_count_ref[u], prob_ref[own, :] - mass, 0.0)
        logit_ref[own, :] = kept.astype(jnp.bfloat16)
def binary_digits(axis, count):
    index = lax.axis_index(axis)
    digits = []
    step = 1
    while step < count:
        digit = lax.rem(index // step, 2)
        digits.append((axis, digit, index + step * (1 - 2 * digit)))
        step *= 2
    return digits


def halving_plan(seq_count, dp_count):
    seq_bits = [("seq", i) for i in range(seq_count.bit_length() - 1)]
    dp_bits = [("dp", i) for i in range(dp_count.bit_length() - 1)]
    first, others = seq_bits[:1], seq_bits[1:]
    along = first + others + dp_bits
    across = first + dp_bits[:1] + others + dp_bits[1:]
    held = others[::-1] + dp_bits[::-1]
    return held, (along, across)


def row_chunks(rows):
    quarter = -(-rows // 10 // 8) * 8
    return [(low, min(quarter, rows - low)) for low in range(0, rows, quarter)]


def fused_kernel(seq_count, dp_count, label_count_ref, frame_count_ref, enc_ref, weight_ref,
                 labels_ref, logit_ref, row_ref, out_ref, prob_ref, gathered_ref, hot_ref, table_ref,
                 turned_ref, ahead_ref, back_ref, mass_ref, sent_ref, kept_ref, share_send, share_recv,
                 send_sems, recv_sems, *landed):
    me = lax.axis_index("seq")
    digits = {
        (axis, i): entry
        for axis, count in (("seq", seq_count), ("dp", dp_count))
        for i, entry in enumerate(binary_digits(axis, count))
    }
    greeted = [("seq", lax.rem(me + step, seq_count)) for step in range(1, seq_count)]
    greeted += [(axis, partner) for axis, _, partner in digits.values() if axis == "dp"]
    barrier = pltpu.get_barrier_semaphore()
    for axis, partner in greeted:
        pl.semaphore_signal(barrier, inc=1, device_id={axis: partner}, device_id_type=MESH)

    def before_sending():
        pl.semaphore_wait(barrier, len(greeted))

    def meanwhile():
        turned_ref[...] = jnp.transpose(enc_ref[...])

    share_emissions(seq_count, enc_ref, weight_ref, labels_ref, prob_ref, gathered_ref, hot_ref,
                    table_ref, share_send, share_recv, before_sending, meanwhile)
    lattice_gradients(label_count_ref, frame_count_ref, gathered_ref, labels_ref, prob_ref, hot_ref,
                      logit_ref, table_ref, ahead_ref, back_ref, mass_ref)

    grad = logit_ref[...]
    columns = sent_ref.shape[-1]
    core = digits[("seq", 0)][1]
    even = [grad[:, s * columns:(s + 1) * columns] for s in range(0, seq_count, 2)]
    odd = [grad[:, s * columns:(s + 1) * columns] for s in range(1, seq_count, 2)]

    def fill(target_ref, halves):
        product = jnp.dot(
            turned_ref[...], jnp.concatenate(halves, axis=1), preferred_element_type=jnp.float32
        )
        high = (seq_count // 2).bit_length() - 1
        for h in range(seq_count // 2):
            place = tuple((h >> (high - 1 - i)) & 1 for i in range(high))
            piece = product[:, h * columns:(h + 1) * columns]
            target_ref[place] = piece.reshape(target_ref.shape[high:])

    first = core == 0
    fill(sent_ref, [jnp.where(first, o, e) for e, o in zip(even, odd)])

    held, orders = halving_plan(seq_count, dp_count)
    rows = out_ref.shape[0]
    chunks = row_chunks(rows)
    stages = len(held) + 1
    landing = [landed[c * stages:(c + 1) * stages] for c in range(len(chunks))]
    names = [list(held) for _ in chunks]
    pending = [None] * len(chunks)

    def dense(ref, low, size):
        return ref.at[(slice(None),) * len(held) + (pl.ds(low, size),)]

    def launch(c, stage, source, kept, bit):
        axis, _, partner = digits[bit]
        copy = pltpu.make_async_remote_copy(
            src_ref=source,
            dst_ref=landing[c][stage],
            send_sem=send_sems.at[c, stage],
            recv_sem=recv_sems.at[c, stage],
            device_id={axis: partner},
            device_id_type=MESH,
        )
        copy.start()
        pending[c] = (copy, kept)

    for c, (low, size) in enumerate(chunks):
        launch(c, 0, dense(sent_ref, low, size), dense(kept_ref, low, size), ("seq", 0))
    fill(kept_ref, [jnp.where(first, e, o) for e, o in zip(even, odd)])
    row_ref[...] = lax.dot_general(
        grad, weight_ref[...], BOTH_LAST, preferred_element_type=jnp.float32
    ).astype(jnp.bfloat16)
    for stage in range(1, stages):
        for c in range(len(chunks)):
            copy, kept = pending[c]
            copy.wait()
            current = landing[c][stage - 1]
            current[...] += kept[...]
            bit = orders[c % 2][stage]
            ahead = (slice(None),) * names[c].index(bit)
            names[c].remove(bit)
            digit = digits[bit][1]
            launch(c, stage, current.at[ahead + (1 - digit,)], current.at[ahead + (digit,)], bit)
    for c, (low, size) in enumerate(chunks):
        copy, kept = pending[c]
        copy.wait()
        total = landing[c][stages - 1][...] + kept[...]
        out_ref[low:low + size] = total / (dp_count * labels_ref.shape[0])


def shards(enc_rows, out_weight, labels, label_count, frame_count):
    utterances, frames, width = enc_rows.shape
    vocabulary = out_weight.shape[1]
    length = labels.shape[1]
    slots = length + 1
    pack = LANES // slots
    groups = utterances // pack
    seq_count = lax.axis_size("seq")
    flat_rows = enc_rows.reshape(utterances * frames, width)
    vmem = pl.BlockSpec(memory_space=pltpu.VMEM)

    rows = 2 * utterances
    steps = seq_count * frames
    dp_count = lax.axis_size("dp")
    held = halving_plan(seq_count, dp_count)[0]
    block_rows, block_columns = width // dp_count, vocabulary // seq_count
    whole_block = (2,) * len(held) + (block_rows, block_columns)
    chunks = row_chunks(block_rows)
    landed = [
        pltpu.VMEM((2,) * (len(held) - stage) + (size, block_columns), jnp.float32)
        for low, size in chunks
        for stage in range(len(held) + 1)
    ]
    smem = pl.BlockSpec(memory_space=pltpu.SMEM)
    logit_grad, row_grad, weight_grad = pl.pallas_call(
        functools.partial(fused_kernel, seq_count, dp_count),
        out_shape=(
            jax.ShapeDtypeStruct((utterances * frames, vocabulary), jnp.bfloat16),
            jax.ShapeDtypeStruct((utterances * frames, width), jnp.bfloat16),
            jax.ShapeDtypeStruct((block_rows, block_columns), jnp.float32),
        ),
        in_specs=[smem, smem] + [vmem] * 3,
        out_specs=(vmem, vmem, vmem),
        scratch_shapes=[
            pltpu.VMEM((utterances * frames, vocabulary), jnp.float32),
            pltpu.VMEM((groups, steps, LANES), jnp.float32),
            pltpu.VMEM((groups, LANES, vocabulary), jnp.bfloat16),
            pltpu.VMEM((rows, LANES), jnp.int32),
            pltpu.VMEM((width, utterances * frames), jnp.bfloat16),
            pltpu.VMEM((4 * SPLIT, steps * rows, LANES), jnp.float32),
            pltpu.VMEM((4 * SPLIT, steps * rows, LANES), jnp.float32),
            pltpu.VMEM((utterances * frames, LANES), jnp.float32),
            pltpu.VMEM(whole_block, jnp.float32),
            pltpu.VMEM(whole_block, jnp.float32),
            pltpu.SemaphoreType.DMA((seq_count - 1,)),
            pltpu.SemaphoreType.DMA((seq_count - 1,)),
            pltpu.SemaphoreType.DMA((len(chunks), len(held) + 1)),
            pltpu.SemaphoreType.DMA((len(chunks), len(held) + 1)),
        ] + landed,
        compiler_params=pltpu.CompilerParams(
            collective_id=0, has_side_effects=True, vmem_limit_bytes=60 * 1024 * 1024
        ),
        name="fused",
    )(label_count, frame_count, flat_rows, out_weight, labels)
    return (
        logit_grad.reshape(utterances, frames, vocabulary),
        row_grad.reshape(utterances, frames, width),
        weight_grad,
    )


def solution(mesh):
    placed = (P("dp", "seq", None), P(), P("dp", None), P("dp"), P("dp"))
    return jax.shard_map(
        shards,
        mesh=mesh,
        in_specs=placed,
        out_specs=(P("dp", "seq", None), P("dp", "seq", None), P("dp", "seq")),
        check_vma=False,
    )
```

```python
import functools

import jax
import jax.numpy as jnp
from jax import lax
from jax.experimental import pallas as pl
from jax.experimental.pallas import tpu as pltpu
from jax.sharding import PartitionSpec as P

negative_fill = -1e30
LOG2_E = 1.4426950408889634
LANES = 128
SUBLANES = 8
SPLIT = 4
UNROLL = 32
MESH = pl.DeviceIdType.MESH
BOTH_LAST = (((1,), (1,)), ((), ()))


def three_parts(values):
    high = values.astype(jnp.bfloat16)
    rest = values - high.astype(jnp.float32)
    middle = rest.astype(jnp.bfloat16)
    low = (rest - middle.astype(jnp.float32)).astype(jnp.bfloat16)
    return high, middle, low


def label_table(labels_ref, table_ref):
    utterances, length = labels_ref.shape
    table_ref[...] = jnp.zeros_like(table_ref)
    table_ref[0:utterances, 0:length] = labels_ref[...]
    table_ref[utterances:2 * utterances, 0:length] = labels_ref[...]
    return table_ref[...]


def take_lanes(values, index):
    return jnp.take_along_axis(values, index, axis=1)


def character_tables(labels_ref, table_ref, hot_ref):
    groups, _, vocabulary = hot_ref.shape
    utterances, length = labels_ref.shape
    slots = length + 1
    pack = utterances // groups
    width = slots // SPLIT
    table = label_table(labels_ref, table_ref)
    lane = lax.broadcasted_iota(jnp.int32, table.shape, 1)
    within = lax.rem(lane, slots)
    order = lax.rem(within, width) * SPLIT + within // width
    chars = take_lanes(table, order).astype(jnp.float32)
    row_lane = lax.broadcasted_iota(jnp.int32, (1, LANES), 1)
    columns = lax.broadcasted_iota(jnp.int32, (LANES, LANES), 1).astype(jnp.float32)
    for group in range(groups):
        first = group * pack
        line = chars[first:first + 1, :]
        for inner in range(1, pack):
            line = jnp.where(row_lane >= inner * slots, chars[first + inner:first + inner + 1, :], line)
        down = jnp.transpose(jnp.broadcast_to(line, (LANES, LANES)))
        for low in range(0, vocabulary, LANES):
            hot_ref[group, :, low:low + LANES] = jnp.where(
                down == columns + float(low), 1.0, 0.0
            ).astype(jnp.bfloat16)


def share_emissions(seq_count, enc_ref, weight_ref, labels_ref, prob_ref, gathered_ref, hot_ref,
                    table_ref, send_sems, recv_sems, before_sending, meanwhile):
    utterances, length = labels_ref.shape
    me = lax.axis_index("seq")
    frames = enc_ref.shape[0] // utterances
    groups = gathered_ref.shape[0]
    pack = utterances // groups
    slots = length + 1
    own = pl.ds(pl.multiple_of(me * frames, frames), frames)
    character_tables(labels_ref, table_ref, hot_ref)
    logits = jnp.dot(enc_ref[...], weight_ref[...], preferred_element_type=jnp.float32)
    highest = jnp.max(logits, axis=1, keepdims=True)
    shifted = logits - highest
    powers = jnp.exp(shifted)
    total = jnp.sum(powers, axis=1, keepdims=True)
    logprob = shifted - jnp.log(total)
    prob_ref[...] = powers * (1.0 / total)
    lane = lax.broadcasted_iota(jnp.int32, (frames, LANES), 1)
    for group in range(groups):
        rows = pack * frames
        mine = logprob[group * rows:(group + 1) * rows]
        picked = None
        for part in three_parts(mine):
            product = lax.dot_general(part, hot_ref[group], BOTH_LAST, preferred_element_type=jnp.float32)
            picked = product if picked is None else picked + product
        packed = picked[:frames]
        for inner in range(1, pack):
            packed = jnp.where(lane >= inner * slots, picked[inner * frames:(inner + 1) * frames], packed)
        gathered_ref[group, own, :] = packed * LOG2_E
    before_sending()
    copies = []
    for step in range(1, seq_count):
        peer = lax.rem(me + step, seq_count)
        copy = pltpu.make_async_remote_copy(
            src_ref=gathered_ref.at[:, own],
            dst_ref=gathered_ref.at[:, own],
            send_sem=send_sems.at[step - 1],
            recv_sem=recv_sems.at[step - 1],
            device_id={"seq": peer},
            device_id_type=MESH,
        )
        copy.start()
        copies.append(copy)
    meanwhile()
    for copy in copies:
        copy.wait()


def spread(count_ref, utterance):
    values = jnp.full(utterance.shape, count_ref[0], jnp.int32)
    for u in range(1, count_ref.shape[0]):
        values = jnp.where(utterance == u, count_ref[u], values)
    return values


def lattice_gradients(label_count_ref, frame_count_ref, gathered_ref, labels_ref, prob_ref, hot_ref,
                      logit_ref, table_ref, ahead_ref, back_ref, mass_ref):
    utterances, length = labels_ref.shape
    groups, steps = gathered_ref.shape[:2]
    frames = prob_ref.shape[0] // utterances
    rows = 2 * utterances
    stored = 4 * SPLIT * rows
    slots = length + 1
    width = slots // SPLIT
    pack = utterances // groups
    span = LANES * SPLIT
    shape = (rows, LANES)
    row = lax.broadcasted_iota(jnp.int32, shape, 0)
    lane = lax.broadcasted_iota(jnp.int32, shape, 1)
    forward = row < utterances
    utterance = lax.rem(row, utterances)
    offset = lax.rem(utterance, pack) * slots
    label_rows = table_ref[...]
    label_count = spread(label_count_ref, utterance)
    frame_count = spread(frame_count_ref, utterance)
    first_usable = jnp.where(forward, 0, steps - frame_count)

    label_fill, jump_fill, label_start, blank_start = [], [], [], []
    for r in range(SPLIT):
        run = jnp.where(forward, r, SPLIT - 1 - r)
        j = lane * SPLIT + run
        real = j < length
        label_fill.append(jnp.where(real, 0.0, negative_fill))
        before = jnp.where(forward, j - 1, j + 1)
        here_char = take_lanes(label_rows, jnp.clip(j, 0, LANES - 1))
        before_char = take_lanes(label_rows, jnp.clip(before, 0, LANES - 1))
        can_jump = real & (before >= 0) & (before < length) & (here_char != before_char)
        jump_fill.append(jnp.where(can_jump, 0.0, negative_fill))
        label_begin = j == jnp.where(forward, 0, label_count - 1)
        label_start.append(jnp.where(label_begin, 0.0, negative_fill))
        blank = jnp.where(forward, j, lax.rem(j + 1, span))
        blank_begin = blank == jnp.where(forward, 0, label_count)
        blank_start.append(jnp.where(blank_begin, 0.0, negative_fill))
    blank_index = offset + slots - 1
    inner_of = lax.rem(utterance, pack)
    row_group = utterance // pack

    def frame_row(group, step):
        return jnp.broadcast_to(gathered_ref[group, pl.ds(step, 1), :], shape)

    def raw_emission(step):
        raw = None
        for group in range(groups):
            early = frame_row(group, step)
            late = frame_row(group, steps - 1 - step)
            both = jnp.where(forward, early, late)
            raw = both if raw is None else jnp.where(row_group == group, both, raw)
        return raw

    def label_emissions(raw):
        turned = {}
        for begin in range(0, pack * slots, width):
            turned[begin] = pltpu.roll(raw, LANES - begin, 1) if begin else raw
        found = []
        for r in range(SPLIT):
            chosen = None
            for inner in range(pack):
                ahead = turned[inner * slots + r * width]
                back = turned[inner * slots + (SPLIT - 1 - r) * width]
                both = jnp.where(forward, ahead, back)
                chosen = both if chosen is None else jnp.where(inner_of == inner, both, chosen)
            found.append(chosen + label_fill[r])
        return found

    def behind(values):
        return jnp.where(forward, pltpu.roll(values, 1, 1), pltpu.roll(values, LANES - 1, 1))

    def one_step(step, ahead_slot, back_slot, state, resets):
        labels_v, blanks_v, labels_x, blanks_x = state
        raw = raw_emission(step)
        blank_emission = take_lanes(raw, blank_index)
        label_emission = label_emissions(raw)
        ahead_row = pl.multiple_of(ahead_slot * stored, rows)
        back_row = pl.multiple_of(back_slot * stored, rows)
        full_labels, full_blanks = [], []
        for r in range(SPLIT):
            full_labels.append(labels_v[r] + label_emission[r])
            full_blanks.append(blanks_v[r] + blank_emission)
            ahead_ref[pl.ds(ahead_row + (r) * rows, rows), :] = full_labels[r]
            ahead_ref[pl.ds(ahead_row + (SPLIT + r) * rows, rows), :] = full_blanks[r]
            ahead_ref[pl.ds(ahead_row + (2 * SPLIT + r) * rows, rows), :] = labels_x[r]
            ahead_ref[pl.ds(ahead_row + (3 * SPLIT + r) * rows, rows), :] = blanks_x[r]
            back_ref[pl.ds(back_row + (r) * rows, rows), :] = labels_v[r]
            back_ref[pl.ds(back_row + (SPLIT + r) * rows, rows), :] = blanks_v[r]
            back_ref[pl.ds(back_row + (2 * SPLIT + r) * rows, rows), :] = labels_x[r]
            back_ref[pl.ds(back_row + (3 * SPLIT + r) * rows, rows), :] = blanks_x[r]
        if resets:
            usable = step >= first_usable
        next_labels_v, next_blanks_v, next_labels_x, next_blanks_x = [], [], [], []
        for r in range(SPLIT):
            if r == 0:
                behind_v = behind(full_labels[SPLIT - 1])
                behind_x = behind(labels_x[SPLIT - 1])
            else:
                behind_v = full_labels[r - 1]
                behind_x = labels_x[r - 1]
            jump_v = behind_v + jump_fill[r]
            pivot = jnp.maximum(jnp.maximum(full_blanks[r], full_labels[r]), jump_v)
            fresh_x = (
                jnp.exp2(full_labels[r] - pivot) * labels_x[r]
                + jnp.exp2(full_blanks[r] - pivot) * blanks_x[r]
                + jnp.exp2(jump_v - pivot) * behind_x
            )
            if resets:
                pivot = jnp.where(usable, pivot, label_start[r])
                fresh_x = jnp.where(usable, fresh_x, 1.0)
            next_labels_v.append(pivot)
            next_labels_x.append(fresh_x)
            pivot = jnp.maximum(full_blanks[r], behind_v)
            fresh_x = (
                jnp.exp2(full_blanks[r] - pivot) * blanks_x[r]
                + jnp.exp2(behind_v - pivot) * behind_x
            )
            if resets:
                pivot = jnp.where(usable, pivot, blank_start[r])
                fresh_x = jnp.where(usable, fresh_x, 1.0)
            next_blanks_v.append(pivot)
            next_blanks_x.append(fresh_x)
        return (tuple(next_labels_v), tuple(next_blanks_v), tuple(next_labels_x), tuple(next_blanks_x))

    ones = (jnp.ones(shape, jnp.float32),) * SPLIT

    me = lax.axis_index("seq")
    seq_count = steps // frames

    def history_slot(frame):
        away = lax.rem(frame // frames - me + seq_count, seq_count)
        return (away + seq_count - 1) // seq_count * frames + lax.rem(frame, frames)

    def run_block(resets, block, state):
        labels_v, blanks_v = state
        full = (labels_v, blanks_v, ones, ones)
        ahead_slot = history_slot(block * UNROLL)
        back_slot = history_slot(steps - (block + 1) * UNROLL)
        for inner in range(UNROLL):
            full = one_step(
                block * UNROLL + inner, ahead_slot + inner, back_slot + UNROLL - 1 - inner, full, resets
            )
        labels_v, blanks_v, labels_x, blanks_x = full
        labels_v = tuple(v + jnp.log2(x) for v, x in zip(labels_v, labels_x))
        blanks_v = tuple(v + jnp.log2(x) for v, x in zip(blanks_v, blanks_x))
        return labels_v, blanks_v

    blocks = steps // UNROLL
    resetting = (steps // 2) // UNROLL
    state = (tuple(label_start), tuple(blank_start))
    state = lax.fori_loop(0, resetting, functools.partial(run_block, True), state)
    lax.fori_loop(resetting, blocks, functools.partial(run_block, False), state)

    start = me * frames
    inner_frame = row // utterances

    def posterior_block(block, carry):
        for pair in range(0, SUBLANES, 2):
            low = block * SUBLANES + pair
            first = pl.multiple_of(low * stored, rows)

            def ahead(index):
                return jnp.where(
                    forward, ahead_ref[pl.ds(first + index * rows, rows), :],
                    ahead_ref[pl.ds(first + stored + index * rows - utterances, rows), :],
                )

            def back(index):
                return jnp.where(
                    forward, back_ref[pl.ds(first + index * rows + utterances, rows), :],
                    back_ref[pl.ds(first + stored + index * rows, rows), :],
                )

            def term(ahead_index, back_index, turn):
                level, factor = back(back_index), back(2 * SPLIT + back_index)
                if turn:
                    level, factor = pltpu.roll(level, 1, 1), pltpu.roll(factor, 1, 1)
                factor = factor * ahead(2 * SPLIT + ahead_index)
                return (ahead(ahead_index) + level) + jnp.log2(factor)

            terms = [term(r, SPLIT - 1 - r, False) for r in range(SPLIT)]
            terms += [term(SPLIT + r, SPLIT + (SPLIT - r) % SPLIT, r == 0) for r in range(SPLIT)]
            highest = jnp.max(functools.reduce(jnp.maximum, terms), axis=1, keepdims=True)
            powers = [jnp.exp2(value - highest) for value in terms]
            blank_mass = jnp.sum(functools.reduce(jnp.add, powers[SPLIT:]), axis=1, keepdims=True)
            total = blank_mass + jnp.sum(functools.reduce(jnp.add, powers[:SPLIT]), axis=1, keepdims=True)
            usable = start + low + inner_frame < frame_count
            scale = jnp.where(usable, 1.0 / total, 0.0)
            mass = jnp.where(lane == offset + slots - 1, blank_mass, 0.0)
            for inner in range(pack):
                spread_out = None
                for r in range(SPLIT):
                    shift = inner * slots + r * width
                    moved = pltpu.roll(powers[r], shift, 1) if shift else powers[r]
                    spread_out = moved if spread_out is None else spread_out + moved
                mass += spread_out if pack == 1 else jnp.where(inner_of == inner, spread_out, 0.0)
            mass_ref[pl.ds(pl.multiple_of(low * utterances, rows), rows), :] = mass * scale
        return carry

    lax.fori_loop(0, frames // SUBLANES, posterior_block, 0)

    times = start + lax.broadcasted_iota(jnp.int32, (frames, 1), 0)
    for u in range(utterances):
        own = slice(u * frames, (u + 1) * frames)
        hot = hot_ref[u // pack]
        mass = None
        for part in three_parts(mass_ref[pl.ds(u, frames, stride=utterances), :])[:2]:
            product = jnp.dot(part, hot, preferred_element_type=jnp.float32)
            mass = product if mass is None else mass + product
        kept = jnp.where(times < frame_count_ref[u], prob_ref[own, :] - mass, 0.0)
        logit_ref[own, :] = kept.astype(jnp.bfloat16)
def binary_digits(axis, count):
    index = lax.axis_index(axis)
    digits = []
    step = 1
    while step < count:
        digit = lax.rem(index // step, 2)
        digits.append((axis, digit, index + step * (1 - 2 * digit)))
        step *= 2
    return digits


def halving_plan(seq_count, dp_count):
    seq_bits = [("seq", i) for i in range(seq_count.bit_length() - 1)]
    dp_bits = [("dp", i) for i in range(dp_count.bit_length() - 1)]
    first, others = seq_bits[:1], seq_bits[1:]
    along = first + others + dp_bits
    across = first + dp_bits[:1] + others + dp_bits[1:]
    held = others[::-1] + dp_bits[::-1]
    return held, (along, across)


def row_chunks(rows):
    quarter = -(-rows // 10 // 8) * 8
    return [(low, min(quarter, rows - low)) for low in range(0, rows, quarter)]


def fused_kernel(seq_count, dp_count, label_count_ref, frame_count_ref, enc_ref, weight_ref,
                 labels_ref, logit_ref, row_ref, out_ref, prob_ref, gathered_ref, hot_ref, table_ref,
                 turned_ref, ahead_ref, back_ref, mass_ref, sent_ref, kept_ref, share_send, share_recv,
                 send_sems, recv_sems, *landed):
    me = lax.axis_index("seq")
    digits = {
        (axis, i): entry
        for axis, count in (("seq", seq_count), ("dp", dp_count))
        for i, entry in enumerate(binary_digits(axis, count))
    }
    greeted = [("seq", lax.rem(me + step, seq_count)) for step in range(1, seq_count)]
    greeted += [(axis, partner) for axis, _, partner in digits.values() if axis == "dp"]
    barrier = pltpu.get_barrier_semaphore()
    for axis, partner in greeted:
        pl.semaphore_signal(barrier, inc=1, device_id={axis: partner}, device_id_type=MESH)

    def before_sending():
        pl.semaphore_wait(barrier, len(greeted))

    def meanwhile():
        turned_ref[...] = jnp.transpose(enc_ref[...])

    share_emissions(seq_count, enc_ref, weight_ref, labels_ref, prob_ref, gathered_ref, hot_ref,
                    table_ref, share_send, share_recv, before_sending, meanwhile)
    lattice_gradients(label_count_ref, frame_count_ref, gathered_ref, labels_ref, prob_ref, hot_ref,
                      logit_ref, table_ref, ahead_ref, back_ref, mass_ref)

    grad = logit_ref[...]
    columns = sent_ref.shape[-1]
    core = digits[("seq", 0)][1]
    even = [grad[:, s * columns:(s + 1) * columns] for s in range(0, seq_count, 2)]
    odd = [grad[:, s * columns:(s + 1) * columns] for s in range(1, seq_count, 2)]

    def fill(target_ref, halves):
        product = jnp.dot(
            turned_ref[...], jnp.concatenate(halves, axis=1), preferred_element_type=jnp.float32
        )
        high = (seq_count // 2).bit_length() - 1
        for h in range(seq_count // 2):
            place = tuple((h >> (high - 1 - i)) & 1 for i in range(high))
            piece = product[:, h * columns:(h + 1) * columns]
            target_ref[place] = piece.reshape(target_ref.shape[high:])

    first = core == 0
    fill(sent_ref, [jnp.where(first, o, e) for e, o in zip(even, odd)])

    held, orders = halving_plan(seq_count, dp_count)
    rows = out_ref.shape[0]
    chunks = row_chunks(rows)
    stages = len(held) + 1
    landing = [landed[c * stages:(c + 1) * stages] for c in range(len(chunks))]
    names = [list(held) for _ in chunks]
    pending = [None] * len(chunks)

    def dense(ref, low, size):
        return ref.at[(slice(None),) * len(held) + (pl.ds(low, size),)]

    def launch(c, stage, source, kept, bit):
        axis, _, partner = digits[bit]
        copy = pltpu.make_async_remote_copy(
            src_ref=source,
            dst_ref=landing[c][stage],
            send_sem=send_sems.at[c, stage],
            recv_sem=recv_sems.at[c, stage],
            device_id={axis: partner},
            device_id_type=MESH,
        )
        copy.start()
        pending[c] = (copy, kept)

    for c, (low, size) in enumerate(chunks):
        launch(c, 0, dense(sent_ref, low, size), dense(kept_ref, low, size), ("seq", 0))
    fill(kept_ref, [jnp.where(first, e, o) for e, o in zip(even, odd)])
    row_ref[...] = lax.dot_general(
        grad, weight_ref[...], BOTH_LAST, preferred_element_type=jnp.float32
    ).astype(jnp.bfloat16)
    for stage in range(1, stages):
        for c in range(len(chunks)):
            copy, kept = pending[c]
            copy.wait()
            current = landing[c][stage - 1]
            current[...] += kept[...]
            bit = orders[c % 2][stage]
            ahead = (slice(None),) * names[c].index(bit)
            names[c].remove(bit)
            digit = digits[bit][1]
            launch(c, stage, current.at[ahead + (1 - digit,)], current.at[ahead + (digit,)], bit)
    for c, (low, size) in enumerate(chunks):
        copy, kept = pending[c]
        copy.wait()
        total = landing[c][stages - 1][...] + kept[...]
        out_ref[low:low + size] = total / (dp_count * labels_ref.shape[0])


def write_results(*refs):
    sems = refs[-1]
    count = (len(refs) - 1) // 2
    copies = [
        pltpu.make_async_copy(refs[i], refs[count + i], sems.at[i]) for i in range(count)
    ]
    for copy in copies:
        copy.start()
    for copy in copies:
        copy.wait()


def shards(enc_rows, out_weight, labels, label_count, frame_count):
    utterances, frames, width = enc_rows.shape
    vocabulary = out_weight.shape[1]
    length = labels.shape[1]
    slots = length + 1
    pack = LANES // slots
    groups = utterances // pack
    seq_count = lax.axis_size("seq")
    flat_rows = enc_rows.reshape(utterances * frames, width)
    vmem = pl.BlockSpec(memory_space=pltpu.VMEM)

    rows = 2 * utterances
    steps = seq_count * frames
    dp_count = lax.axis_size("dp")
    held = halving_plan(seq_count, dp_count)[0]
    block_rows, block_columns = width // dp_count, vocabulary // seq_count
    whole_block = (2,) * len(held) + (block_rows, block_columns)
    chunks = row_chunks(block_rows)
    landed = [
        pltpu.VMEM((2,) * (len(held) - stage) + (size, block_columns), jnp.float32)
        for low, size in chunks
        for stage in range(len(held) + 1)
    ]
    smem = pl.BlockSpec(memory_space=pltpu.SMEM)
    logit_grad, row_grad, weight_grad = pl.pallas_call(
        functools.partial(fused_kernel, seq_count, dp_count),
        out_shape=(
            pltpu.VMEM((utterances * frames, vocabulary), jnp.bfloat16),
            pltpu.VMEM((utterances * frames, width), jnp.bfloat16),
            pltpu.VMEM((block_rows, block_columns), jnp.float32),
        ),
        in_specs=[smem, smem] + [vmem] * 3,
        out_specs=(vmem, vmem, vmem),
        scratch_shapes=[
            pltpu.VMEM((utterances * frames, vocabulary), jnp.float32),
            pltpu.VMEM((groups, steps, LANES), jnp.float32),
            pltpu.VMEM((groups, LANES, vocabulary), jnp.bfloat16),
            pltpu.VMEM((rows, LANES), jnp.int32),
            pltpu.VMEM((width, utterances * frames), jnp.bfloat16),
            pltpu.VMEM((2 * frames * 4 * SPLIT * rows, LANES), jnp.float32),
            pltpu.VMEM((2 * frames * 4 * SPLIT * rows, LANES), jnp.float32),
            pltpu.VMEM((utterances * frames, LANES), jnp.float32),
            pltpu.VMEM(whole_block, jnp.float32),
            pltpu.VMEM(whole_block, jnp.float32),
            pltpu.SemaphoreType.DMA((seq_count - 1,)),
            pltpu.SemaphoreType.DMA((seq_count - 1,)),
            pltpu.SemaphoreType.DMA((len(chunks), len(held) + 1)),
            pltpu.SemaphoreType.DMA((len(chunks), len(held) + 1)),
        ] + landed,
        compiler_params=pltpu.CompilerParams(
            collective_id=0, has_side_effects=True, vmem_limit_bytes=60 * 1024 * 1024
        ),
        name="fused",
    )(label_count, frame_count, flat_rows, out_weight, labels)
    logit_grad, row_grad, weight_grad = pl.pallas_call(
        write_results,
        out_shape=(
            jax.ShapeDtypeStruct((utterances * frames, vocabulary), jnp.bfloat16),
            jax.ShapeDtypeStruct((utterances * frames, width), jnp.bfloat16),
            jax.ShapeDtypeStruct((block_rows, block_columns), jnp.float32),
        ),
        in_specs=[vmem] * 3,
        out_specs=(pl.BlockSpec(memory_space=pl.ANY),) * 3,
        scratch_shapes=[pltpu.SemaphoreType.DMA((3,))],
        compiler_params=pltpu.CompilerParams(vmem_limit_bytes=4 * 1024 * 1024),
        name="write_results",
    )(logit_grad, row_grad, weight_grad)
    return (
        logit_grad.reshape(utterances, frames, vocabulary),
        row_grad.reshape(utterances, frames, width),
        weight_grad,
    )


def solution(mesh):
    placed = (P("dp", "seq", None), P(), P("dp", None), P("dp"), P("dp"))
    return jax.shard_map(
        shards,
        mesh=mesh,
        in_specs=placed,
        out_specs=(P("dp", "seq", None), P("dp", "seq", None), P("dp", "seq")),
        check_vma=False,
    )
```

```python
import functools
import itertools

import jax
import jax.numpy as jnp
from jax import lax
from jax.experimental import pallas as pl
from jax.experimental.pallas import tpu as pltpu
from jax.sharding import PartitionSpec as P

negative_fill = -1e30
LOG2_E = 1.4426950408889634
LANES = 128
SUBLANES = 8
SPLIT = 4
UNROLL = 32
MESH = pl.DeviceIdType.MESH
BOTH_LAST = (((1,), (1,)), ((), ()))


def three_parts(values):
    high = values.astype(jnp.bfloat16)
    rest = values - high.astype(jnp.float32)
    middle = rest.astype(jnp.bfloat16)
    low = (rest - middle.astype(jnp.float32)).astype(jnp.bfloat16)
    return high, middle, low


def label_table(labels_ref, table_ref):
    utterances, length = labels_ref.shape
    table_ref[...] = jnp.zeros_like(table_ref)
    table_ref[0:utterances, 0:length] = labels_ref[...]
    table_ref[utterances:2 * utterances, 0:length] = labels_ref[...]
    return table_ref[...]


def take_lanes(values, index):
    return jnp.take_along_axis(values, index, axis=1)


def character_tables(labels_ref, table_ref, hot_ref):
    groups, _, vocabulary = hot_ref.shape
    utterances, length = labels_ref.shape
    slots = length + 1
    pack = utterances // groups
    width = slots // SPLIT
    table = label_table(labels_ref, table_ref)
    lane = lax.broadcasted_iota(jnp.int32, table.shape, 1)
    within = lax.rem(lane, slots)
    order = lax.rem(within, width) * SPLIT + within // width
    chars = take_lanes(table, order).astype(jnp.float32)
    row_lane = lax.broadcasted_iota(jnp.int32, (1, LANES), 1)
    columns = lax.broadcasted_iota(jnp.int32, (LANES, LANES), 1).astype(jnp.float32)
    for group in range(groups):
        first = group * pack
        line = chars[first:first + 1, :]
        for inner in range(1, pack):
            line = jnp.where(row_lane >= inner * slots, chars[first + inner:first + inner + 1, :], line)
        down = jnp.transpose(jnp.broadcast_to(line, (LANES, LANES)))
        for low in range(0, vocabulary, LANES):
            hot_ref[group, :, low:low + LANES] = jnp.where(
                down == columns + float(low), 1.0, 0.0
            ).astype(jnp.bfloat16)


def share_emissions(seq_count, enc_ref, weight_ref, labels_ref, prob_ref, gathered_ref, hot_ref,
                    table_ref, send_sems, recv_sems, before_sending, meanwhile):
    utterances, length = labels_ref.shape
    me = lax.axis_index("seq")
    frames = enc_ref.shape[0] // utterances
    groups = gathered_ref.shape[0]
    pack = utterances // groups
    slots = length + 1
    own = pl.ds(pl.multiple_of(me * frames, frames), frames)
    character_tables(labels_ref, table_ref, hot_ref)
    logits = jnp.dot(enc_ref[...], weight_ref[...], preferred_element_type=jnp.float32)
    highest = jnp.max(logits, axis=1, keepdims=True)
    shifted = logits - highest
    powers = jnp.exp(shifted)
    total = jnp.sum(powers, axis=1, keepdims=True)
    logprob = shifted - jnp.log(total)
    prob_ref[...] = powers * (1.0 / total)
    lane = lax.broadcasted_iota(jnp.int32, (frames, LANES), 1)
    for group in range(groups):
        rows = pack * frames
        mine = logprob[group * rows:(group + 1) * rows]
        picked = None
        for part in three_parts(mine):
            product = lax.dot_general(part, hot_ref[group], BOTH_LAST, preferred_element_type=jnp.float32)
            picked = product if picked is None else picked + product
        packed = picked[:frames]
        for inner in range(1, pack):
            packed = jnp.where(lane >= inner * slots, picked[inner * frames:(inner + 1) * frames], packed)
        gathered_ref[group, own, :] = packed * LOG2_E
    before_sending()
    copies = []
    for step in range(1, seq_count):
        peer = lax.rem(me + step, seq_count)
        copy = pltpu.make_async_remote_copy(
            src_ref=gathered_ref.at[:, own],
            dst_ref=gathered_ref.at[:, own],
            send_sem=send_sems.at[step - 1],
            recv_sem=recv_sems.at[step - 1],
            device_id={"seq": peer},
            device_id_type=MESH,
        )
        copy.start()
        copies.append(copy)
    meanwhile()
    for copy in copies:
        copy.wait()


def spread(count_ref, utterance):
    values = jnp.full(utterance.shape, count_ref[0], jnp.int32)
    for u in range(1, count_ref.shape[0]):
        values = jnp.where(utterance == u, count_ref[u], values)
    return values


def lattice_gradients(label_count_ref, frame_count_ref, gathered_ref, labels_ref, prob_ref, hot_ref,
                      logit_ref, table_ref, ahead_ref, back_ref, mass_ref):
    utterances, length = labels_ref.shape
    groups, steps = gathered_ref.shape[:2]
    frames = prob_ref.shape[0] // utterances
    rows = 2 * utterances
    stored = 4 * SPLIT * rows
    slots = length + 1
    width = slots // SPLIT
    pack = utterances // groups
    span = LANES * SPLIT
    shape = (rows, LANES)
    row = lax.broadcasted_iota(jnp.int32, shape, 0)
    lane = lax.broadcasted_iota(jnp.int32, shape, 1)
    forward = row < utterances
    utterance = lax.rem(row, utterances)
    offset = lax.rem(utterance, pack) * slots
    label_rows = table_ref[...]
    label_count = spread(label_count_ref, utterance)
    frame_count = spread(frame_count_ref, utterance)
    first_usable = jnp.where(forward, 0, steps - frame_count)

    label_fill, jump_fill, label_start, blank_start = [], [], [], []
    for r in range(SPLIT):
        run = jnp.where(forward, r, SPLIT - 1 - r)
        j = lane * SPLIT + run
        real = j < length
        label_fill.append(jnp.where(real, 0.0, negative_fill))
        before = jnp.where(forward, j - 1, j + 1)
        here_char = take_lanes(label_rows, jnp.clip(j, 0, LANES - 1))
        before_char = take_lanes(label_rows, jnp.clip(before, 0, LANES - 1))
        can_jump = real & (before >= 0) & (before < length) & (here_char != before_char)
        jump_fill.append(jnp.where(can_jump, 0.0, negative_fill))
        label_begin = j == jnp.where(forward, 0, label_count - 1)
        label_start.append(jnp.where(label_begin, 0.0, negative_fill))
        blank = jnp.where(forward, j, lax.rem(j + 1, span))
        blank_begin = blank == jnp.where(forward, 0, label_count)
        blank_start.append(jnp.where(blank_begin, 0.0, negative_fill))
    blank_index = offset + slots - 1
    inner_of = lax.rem(utterance, pack)
    row_group = utterance // pack

    def frame_row(group, step):
        return jnp.broadcast_to(gathered_ref[group, pl.ds(step, 1), :], shape)

    def raw_emission(step):
        raw = None
        for group in range(groups):
            early = frame_row(group, step)
            late = frame_row(group, steps - 1 - step)
            both = jnp.where(forward, early, late)
            raw = both if raw is None else jnp.where(row_group == group, both, raw)
        return raw

    def label_emissions(raw):
        turned = {}
        for begin in range(0, pack * slots, width):
            turned[begin] = pltpu.roll(raw, LANES - begin, 1) if begin else raw
        found = []
        for r in range(SPLIT):
            chosen = None
            for inner in range(pack):
                ahead = turned[inner * slots + r * width]
                back = turned[inner * slots + (SPLIT - 1 - r) * width]
                both = jnp.where(forward, ahead, back)
                chosen = both if chosen is None else jnp.where(inner_of == inner, both, chosen)
            found.append(chosen + label_fill[r])
        return found

    def behind(values):
        return jnp.where(forward, pltpu.roll(values, 1, 1), pltpu.roll(values, LANES - 1, 1))

    def one_step(step, ahead_slot, back_slot, state, resets):
        labels_v, blanks_v, labels_x, blanks_x = state
        raw = raw_emission(step)
        blank_emission = take_lanes(raw, blank_index)
        label_emission = label_emissions(raw)
        ahead_row = pl.multiple_of(ahead_slot * stored, rows)
        back_row = pl.multiple_of(back_slot * stored, rows)
        full_labels, full_blanks = [], []
        for r in range(SPLIT):
            full_labels.append(labels_v[r] + label_emission[r])
            full_blanks.append(blanks_v[r] + blank_emission)
            ahead_ref[pl.ds(ahead_row + (r) * rows, rows), :] = full_labels[r]
            ahead_ref[pl.ds(ahead_row + (SPLIT + r) * rows, rows), :] = full_blanks[r]
            ahead_ref[pl.ds(ahead_row + (2 * SPLIT + r) * rows, rows), :] = labels_x[r]
            ahead_ref[pl.ds(ahead_row + (3 * SPLIT + r) * rows, rows), :] = blanks_x[r]
            back_ref[pl.ds(back_row + (r) * rows, rows), :] = labels_v[r]
            back_ref[pl.ds(back_row + (SPLIT + r) * rows, rows), :] = blanks_v[r]
            back_ref[pl.ds(back_row + (2 * SPLIT + r) * rows, rows), :] = labels_x[r]
            back_ref[pl.ds(back_row + (3 * SPLIT + r) * rows, rows), :] = blanks_x[r]
        if resets:
            usable = step >= first_usable
        next_labels_v, next_blanks_v, next_labels_x, next_blanks_x = [], [], [], []
        for r in range(SPLIT):
            if r == 0:
                behind_v = behind(full_labels[SPLIT - 1])
                behind_x = behind(labels_x[SPLIT - 1])
            else:
                behind_v = full_labels[r - 1]
                behind_x = labels_x[r - 1]
            jump_v = behind_v + jump_fill[r]
            pivot = jnp.maximum(jnp.maximum(full_blanks[r], full_labels[r]), jump_v)
            fresh_x = (
                jnp.exp2(full_labels[r] - pivot) * labels_x[r]
                + jnp.exp2(full_blanks[r] - pivot) * blanks_x[r]
                + jnp.exp2(jump_v - pivot) * behind_x
            )
            if resets:
                pivot = jnp.where(usable, pivot, label_start[r])
                fresh_x = jnp.where(usable, fresh_x, 1.0)
            next_labels_v.append(pivot)
            next_labels_x.append(fresh_x)
            pivot = jnp.maximum(full_blanks[r], behind_v)
            fresh_x = (
                jnp.exp2(full_blanks[r] - pivot) * blanks_x[r]
                + jnp.exp2(behind_v - pivot) * behind_x
            )
            if resets:
                pivot = jnp.where(usable, pivot, blank_start[r])
                fresh_x = jnp.where(usable, fresh_x, 1.0)
            next_blanks_v.append(pivot)
            next_blanks_x.append(fresh_x)
        return (tuple(next_labels_v), tuple(next_blanks_v), tuple(next_labels_x), tuple(next_blanks_x))

    ones = (jnp.ones(shape, jnp.float32),) * SPLIT

    me = lax.axis_index("seq")
    seq_count = steps // frames

    def history_slot(frame):
        away = lax.rem(frame // frames - me + seq_count, seq_count)
        return (away + seq_count - 1) // seq_count * frames + lax.rem(frame, frames)

    def run_block(resets, block, state):
        labels_v, blanks_v = state
        full = (labels_v, blanks_v, ones, ones)
        ahead_slot = history_slot(block * UNROLL)
        back_slot = history_slot(steps - (block + 1) * UNROLL)
        for inner in range(UNROLL):
            full = one_step(
                block * UNROLL + inner, ahead_slot + inner, back_slot + UNROLL - 1 - inner, full, resets
            )
        labels_v, blanks_v, labels_x, blanks_x = full
        labels_v = tuple(v + jnp.log2(x) for v, x in zip(labels_v, labels_x))
        blanks_v = tuple(v + jnp.log2(x) for v, x in zip(blanks_v, blanks_x))
        return labels_v, blanks_v

    blocks = steps // UNROLL
    resetting = (steps // 2) // UNROLL
    state = (tuple(label_start), tuple(blank_start))
    state = lax.fori_loop(0, resetting, functools.partial(run_block, True), state)
    lax.fori_loop(resetting, blocks, functools.partial(run_block, False), state)

    start = me * frames
    inner_frame = row // utterances

    def posterior_block(block, carry):
        for pair in range(0, SUBLANES, 2):
            low = block * SUBLANES + pair
            first = pl.multiple_of(low * stored, rows)

            def ahead(index):
                return jnp.where(
                    forward, ahead_ref[pl.ds(first + index * rows, rows), :],
                    ahead_ref[pl.ds(first + stored + index * rows - utterances, rows), :],
                )

            def back(index):
                return jnp.where(
                    forward, back_ref[pl.ds(first + index * rows + utterances, rows), :],
                    back_ref[pl.ds(first + stored + index * rows, rows), :],
                )

            def term(ahead_index, back_index, turn):
                level, factor = back(back_index), back(2 * SPLIT + back_index)
                if turn:
                    level, factor = pltpu.roll(level, 1, 1), pltpu.roll(factor, 1, 1)
                factor = factor * ahead(2 * SPLIT + ahead_index)
                return (ahead(ahead_index) + level) + jnp.log2(factor)

            terms = [term(r, SPLIT - 1 - r, False) for r in range(SPLIT)]
            terms += [term(SPLIT + r, SPLIT + (SPLIT - r) % SPLIT, r == 0) for r in range(SPLIT)]
            highest = jnp.max(functools.reduce(jnp.maximum, terms), axis=1, keepdims=True)
            powers = [jnp.exp2(value - highest) for value in terms]
            blank_mass = jnp.sum(functools.reduce(jnp.add, powers[SPLIT:]), axis=1, keepdims=True)
            total = blank_mass + jnp.sum(functools.reduce(jnp.add, powers[:SPLIT]), axis=1, keepdims=True)
            usable = start + low + inner_frame < frame_count
            scale = jnp.where(usable, 1.0 / total, 0.0)
            mass = jnp.where(lane == offset + slots - 1, blank_mass, 0.0)
            for inner in range(pack):
                spread_out = None
                for r in range(SPLIT):
                    shift = inner * slots + r * width
                    moved = pltpu.roll(powers[r], shift, 1) if shift else powers[r]
                    spread_out = moved if spread_out is None else spread_out + moved
                mass += spread_out if pack == 1 else jnp.where(inner_of == inner, spread_out, 0.0)
            mass_ref[pl.ds(pl.multiple_of(low * utterances, rows), rows), :] = mass * scale
        return carry

    lax.fori_loop(0, frames // SUBLANES, posterior_block, 0)

    times = start + lax.broadcasted_iota(jnp.int32, (frames, 1), 0)
    for u in range(utterances):
        own = slice(u * frames, (u + 1) * frames)
        hot = hot_ref[u // pack]
        mass = None
        for part in three_parts(mass_ref[pl.ds(u, frames, stride=utterances), :])[:2]:
            product = jnp.dot(part, hot, preferred_element_type=jnp.float32)
            mass = product if mass is None else mass + product
        kept = jnp.where(times < frame_count_ref[u], prob_ref[own, :] - mass, 0.0)
        logit_ref[own, :] = kept.astype(jnp.bfloat16)
def binary_digits(axis, count):
    index = lax.axis_index(axis)
    digits = []
    step = 1
    while step < count:
        digit = lax.rem(index // step, 2)
        digits.append((axis, digit, index + step * (1 - 2 * digit)))
        step *= 2
    return digits


def link_bits(seq_count, dp_count):
    seq_bits = [("seq", i) for i in range(1, seq_count.bit_length() - 1)]
    dp_bits = [("dp", i) for i in range(dp_count.bit_length() - 1)]
    return seq_bits, dp_bits


def play(orders, sizes, cost):
    free, arrivals, taken = {}, {}, []
    clock = 0.3
    first_left = len(orders)

    def launch(chunk, stage, begin):
        line, rate, latency = cost(orders[chunk][stage])
        end = max(begin, free.get(line, 0.0)) + sizes[chunk] / 2 ** (stage + 1) / rate
        free[line] = end
        arrivals[chunk] = (end + latency, chunk, stage)

    for chunk in range(len(orders)):
        launch(chunk, 0, 0.0)
    while arrivals:
        arrived, chunk, stage = min(arrivals.values())
        del arrivals[chunk]
        clock = max(clock, arrived) + 0.01 + sizes[chunk] / 2 ** (stage + 1) / 4e6
        taken.append((chunk, stage))
        if stage + 1 < len(orders[chunk]):
            launch(chunk, stage + 1, clock)
        if stage == 0:
            first_left -= 1
            if first_left == 0:
                clock += 0.45
    return clock, taken


def transfer_plan(seq_count, dp_count, sizes):
    seq_bits, dp_bits = link_bits(seq_count, dp_count)
    bits = seq_bits + dp_bits
    core = ("seq", 0)

    def cost(bit):
        axis, i = bit
        if bit == core:
            return "core", 0.4e6, 0.9
        far = 2 ** (i - 1) if i else 1
        line = "seq" if axis == "seq" else ("dp first" if i == 0 else "dp rest")
        return line, 0.05e6 / far, 1.0 + 0.7 * far

    if len(bits) <= 4:
        choices = [(core,) + order for order in itertools.permutations(bits)]
    else:
        choices = [(core,) + tuple(bits[k:] + bits[:k]) for k in range(len(bits))]
    orders = [choices[c % len(choices)] for c in range(len(sizes))]
    best = play(orders, sizes, cost)[0]
    for _ in range(4):
        before = best
        for chunk in range(len(sizes)):
            for choice in choices:
                trial = orders[:chunk] + [choice] + orders[chunk + 1:]
                length = play(trial, sizes, cost)[0]
                if length < best:
                    best, orders = length, trial
        if best == before:
            break
    return orders, play(orders, sizes, cost)[1]


def row_chunks(rows):
    quarter = -(-rows // 10 // 8) * 8
    return [(low, min(quarter, rows - low)) for low in range(0, rows, quarter)]


def fused_kernel(seq_count, dp_count, label_count_ref, frame_count_ref, enc_ref, weight_ref,
                 labels_ref, logit_ref, row_ref, out_ref, prob_ref, gathered_ref, hot_ref, table_ref,
                 turned_ref, ahead_ref, back_ref, mass_ref, sent_ref, kept_ref, share_send, share_recv,
                 send_sems, recv_sems, *landed):
    me = lax.axis_index("seq")
    digits = {
        (axis, i): entry
        for axis, count in (("seq", seq_count), ("dp", dp_count))
        for i, entry in enumerate(binary_digits(axis, count))
    }
    greeted = [("seq", lax.rem(me + step, seq_count)) for step in range(1, seq_count)]
    greeted += [(axis, partner) for axis, _, partner in digits.values() if axis == "dp"]
    barrier = pltpu.get_barrier_semaphore()
    for axis, partner in greeted:
        pl.semaphore_signal(barrier, inc=1, device_id={axis: partner}, device_id_type=MESH)

    def before_sending():
        pl.semaphore_wait(barrier, len(greeted))

    def meanwhile():
        turned_ref[...] = jnp.transpose(enc_ref[...])

    share_emissions(seq_count, enc_ref, weight_ref, labels_ref, prob_ref, gathered_ref, hot_ref,
                    table_ref, share_send, share_recv, before_sending, meanwhile)
    lattice_gradients(label_count_ref, frame_count_ref, gathered_ref, labels_ref, prob_ref, hot_ref,
                      logit_ref, table_ref, ahead_ref, back_ref, mass_ref)

    grad = logit_ref[...]
    columns = sent_ref.shape[-1]
    core = digits[("seq", 0)][1]
    even = [grad[:, s * columns:(s + 1) * columns] for s in range(0, seq_count, 2)]
    odd = [grad[:, s * columns:(s + 1) * columns] for s in range(1, seq_count, 2)]

    def fill(target_ref, halves):
        product = jnp.dot(
            turned_ref[...], jnp.concatenate(halves, axis=1), preferred_element_type=jnp.float32
        )
        high = (seq_count // 2).bit_length() - 1
        for h in range(seq_count // 2):
            place = tuple((h >> (high - 1 - i)) & 1 for i in range(high))
            piece = product[:, h * columns:(h + 1) * columns]
            target_ref[place] = piece.reshape(target_ref.shape[high:])

    first = core == 0
    fill(sent_ref, [jnp.where(first, o, e) for e, o in zip(even, odd)])

    seq_bits, dp_bits = link_bits(seq_count, dp_count)
    held = seq_bits[::-1] + dp_bits[::-1]
    rows = out_ref.shape[0]
    chunks = row_chunks(rows)
    stages = len(held) + 1
    orders, taken = transfer_plan(
        seq_count, dp_count, [size * columns * 2 ** stages * 4 for _, size in chunks]
    )
    landing = [landed[c * stages:(c + 1) * stages] for c in range(len(chunks))]
    names = [list(held) for _ in chunks]
    pending = [None] * len(chunks)

    def dense(ref, low, size):
        return ref.at[(slice(None),) * len(held) + (pl.ds(low, size),)]

    def launch(c, stage, source, kept, bit):
        axis, _, partner = digits[bit]
        copy = pltpu.make_async_remote_copy(
            src_ref=source,
            dst_ref=landing[c][stage],
            send_sem=send_sems.at[c],
            recv_sem=recv_sems.at[c, stage],
            device_id={axis: partner},
            device_id_type=MESH,
        )
        copy.start()
        pending[c] = (copy, kept)

    for c, (low, size) in enumerate(chunks):
        launch(c, 0, dense(sent_ref, low, size), dense(kept_ref, low, size), ("seq", 0))
    fill(kept_ref, [jnp.where(first, e, o) for e, o in zip(even, odd)])
    last_first = max(i for i, (_, stage) in enumerate(taken) if stage == 0)
    for i, (c, stage) in enumerate(taken):
        copy, kept = pending[c]
        copy.wait()
        current = landing[c][stage]
        if stage + 1 < stages:
            current[...] += kept[...]
            bit = orders[c][stage + 1]
            ahead = (slice(None),) * names[c].index(bit)
            names[c].remove(bit)
            digit = digits[bit][1]
            launch(c, stage + 1, current.at[ahead + (1 - digit,)], current.at[ahead + (digit,)], bit)
        else:
            low, size = chunks[c]
            out_ref[low:low + size] = (current[...] + kept[...]) / (dp_count * labels_ref.shape[0])
        if i == last_first:
            row_ref[...] = lax.dot_general(
                grad, weight_ref[...], BOTH_LAST, preferred_element_type=jnp.float32
            ).astype(jnp.bfloat16)


def write_results(*refs):
    sems = refs[-1]
    count = (len(refs) - 1) // 2
    copies = [
        pltpu.make_async_copy(refs[i], refs[count + i], sems.at[i]) for i in range(count)
    ]
    for copy in copies:
        copy.start()
    for copy in copies:
        copy.wait()


def shards(enc_rows, out_weight, labels, label_count, frame_count):
    utterances, frames, width = enc_rows.shape
    vocabulary = out_weight.shape[1]
    length = labels.shape[1]
    slots = length + 1
    pack = LANES // slots
    groups = utterances // pack
    seq_count = lax.axis_size("seq")
    flat_rows = enc_rows.reshape(utterances * frames, width)
    vmem = pl.BlockSpec(memory_space=pltpu.VMEM)

    rows = 2 * utterances
    steps = seq_count * frames
    dp_count = lax.axis_size("dp")
    held = sum(link_bits(seq_count, dp_count), [])
    block_rows, block_columns = width // dp_count, vocabulary // seq_count
    whole_block = (2,) * len(held) + (block_rows, block_columns)
    chunks = row_chunks(block_rows)
    landed = [
        pltpu.VMEM((2,) * (len(held) - stage) + (size, block_columns), jnp.float32)
        for low, size in chunks
        for stage in range(len(held) + 1)
    ]
    smem = pl.BlockSpec(memory_space=pltpu.SMEM)
    logit_grad, row_grad, weight_grad = pl.pallas_call(
        functools.partial(fused_kernel, seq_count, dp_count),
        out_shape=(
            pltpu.VMEM((utterances * frames, vocabulary), jnp.bfloat16),
            pltpu.VMEM((utterances * frames, width), jnp.bfloat16),
            pltpu.VMEM((block_rows, block_columns), jnp.float32),
        ),
        in_specs=[smem, smem] + [vmem] * 3,
        out_specs=(vmem, vmem, vmem),
        scratch_shapes=[
            pltpu.VMEM((utterances * frames, vocabulary), jnp.float32),
            pltpu.VMEM((groups, steps, LANES), jnp.float32),
            pltpu.VMEM((groups, LANES, vocabulary), jnp.bfloat16),
            pltpu.VMEM((rows, LANES), jnp.int32),
            pltpu.VMEM((width, utterances * frames), jnp.bfloat16),
            pltpu.VMEM((2 * frames * 4 * SPLIT * rows, LANES), jnp.float32),
            pltpu.VMEM((2 * frames * 4 * SPLIT * rows, LANES), jnp.float32),
            pltpu.VMEM((utterances * frames, LANES), jnp.float32),
            pltpu.VMEM(whole_block, jnp.float32),
            pltpu.VMEM(whole_block, jnp.float32),
            pltpu.SemaphoreType.DMA((seq_count - 1,)),
            pltpu.SemaphoreType.DMA((seq_count - 1,)),
            pltpu.SemaphoreType.DMA((len(chunks),)),
            pltpu.SemaphoreType.DMA((len(chunks), len(held) + 1)),
        ] + landed,
        compiler_params=pltpu.CompilerParams(
            collective_id=0, has_side_effects=True, vmem_limit_bytes=60 * 1024 * 1024
        ),
        name="fused",
    )(label_count, frame_count, flat_rows, out_weight, labels)
    logit_grad, row_grad, weight_grad = pl.pallas_call(
        write_results,
        out_shape=(
            jax.ShapeDtypeStruct((utterances * frames, vocabulary), jnp.bfloat16),
            jax.ShapeDtypeStruct((utterances * frames, width), jnp.bfloat16),
            jax.ShapeDtypeStruct((block_rows, block_columns), jnp.float32),
        ),
        in_specs=[vmem] * 3,
        out_specs=(pl.BlockSpec(memory_space=pl.ANY),) * 3,
        scratch_shapes=[pltpu.SemaphoreType.DMA((3,))],
        compiler_params=pltpu.CompilerParams(vmem_limit_bytes=4 * 1024 * 1024),
        name="write_results",
    )(logit_grad, row_grad, weight_grad)
    return (
        logit_grad.reshape(utterances, frames, vocabulary),
        row_grad.reshape(utterances, frames, width),
        weight_grad,
    )


def solution(mesh):
    placed = (P("dp", "seq", None), P(), P("dp", None), P("dp"), P("dp"))
    return jax.shard_map(
        shards,
        mesh=mesh,
        in_specs=placed,
        out_specs=(P("dp", "seq", None), P("dp", "seq", None), P("dp", "seq")),
        check_vma=False,
    )
```

```python
import functools
import itertools

import jax
import jax.numpy as jnp
from jax import lax
from jax.experimental import pallas as pl
from jax.experimental.pallas import tpu as pltpu
from jax.sharding import PartitionSpec as P

negative_fill = -1e30
LOG2_E = 1.4426950408889634
LANES = 128
SUBLANES = 8
SPLIT = 4
UNROLL = 32
JOINED = 2
MESH = pl.DeviceIdType.MESH
BOTH_LAST = (((1,), (1,)), ((), ()))


def three_parts(values):
    high = values.astype(jnp.bfloat16)
    rest = values - high.astype(jnp.float32)
    middle = rest.astype(jnp.bfloat16)
    low = (rest - middle.astype(jnp.float32)).astype(jnp.bfloat16)
    return high, middle, low


def label_table(labels_ref, table_ref):
    utterances, length = labels_ref.shape
    table_ref[...] = jnp.zeros_like(table_ref)
    table_ref[0:utterances, 0:length] = labels_ref[...]
    table_ref[utterances:2 * utterances, 0:length] = labels_ref[...]
    return table_ref[...]


def take_lanes(values, index):
    return jnp.take_along_axis(values, index, axis=1)


def character_tables(labels_ref, table_ref, hot_ref):
    groups, _, vocabulary = hot_ref.shape
    utterances, length = labels_ref.shape
    slots = length + 1
    pack = utterances // groups
    width = slots // SPLIT
    table = label_table(labels_ref, table_ref)
    lane = lax.broadcasted_iota(jnp.int32, table.shape, 1)
    within = lax.rem(lane, slots)
    order = lax.rem(within, width) * SPLIT + within // width
    chars = take_lanes(table, order).astype(jnp.float32)
    row_lane = lax.broadcasted_iota(jnp.int32, (1, LANES), 1)
    columns = lax.broadcasted_iota(jnp.int32, (LANES, LANES), 1).astype(jnp.float32)
    for group in range(groups):
        first = group * pack
        line = chars[first:first + 1, :]
        for inner in range(1, pack):
            line = jnp.where(row_lane >= inner * slots, chars[first + inner:first + inner + 1, :], line)
        down = jnp.transpose(jnp.broadcast_to(line, (LANES, LANES)))
        for low in range(0, vocabulary, LANES):
            hot_ref[group, :, low:low + LANES] = jnp.where(
                down == columns + float(low), 1.0, 0.0
            ).astype(jnp.bfloat16)


def share_emissions(seq_count, enc_ref, weight_ref, labels_ref, prob_ref, gathered_ref, hot_ref,
                    table_ref, send_sems, recv_sems, before_sending, meanwhile):
    utterances, length = labels_ref.shape
    me = lax.axis_index("seq")
    frames = enc_ref.shape[0] // utterances
    groups = gathered_ref.shape[0]
    pack = utterances // groups
    slots = length + 1
    own = pl.ds(pl.multiple_of(me * frames, frames), frames)
    character_tables(labels_ref, table_ref, hot_ref)
    logits = jnp.dot(enc_ref[...], weight_ref[...], preferred_element_type=jnp.float32)
    highest = jnp.max(logits, axis=1, keepdims=True)
    shifted = logits - highest
    powers = jnp.exp(shifted)
    total = jnp.sum(powers, axis=1, keepdims=True)
    logprob = shifted - jnp.log(total)
    prob_ref[...] = powers * (1.0 / total)
    lane = lax.broadcasted_iota(jnp.int32, (frames, LANES), 1)
    for group in range(groups):
        rows = pack * frames
        mine = logprob[group * rows:(group + 1) * rows]
        picked = None
        for part in three_parts(mine):
            product = lax.dot_general(part, hot_ref[group], BOTH_LAST, preferred_element_type=jnp.float32)
            picked = product if picked is None else picked + product
        packed = picked[:frames]
        for inner in range(1, pack):
            packed = jnp.where(lane >= inner * slots, picked[inner * frames:(inner + 1) * frames], packed)
        gathered_ref[group, own, :] = packed * LOG2_E
    before_sending()
    copies = []
    for step in range(1, seq_count):
        peer = lax.rem(me + step, seq_count)
        copy = pltpu.make_async_remote_copy(
            src_ref=gathered_ref.at[:, own],
            dst_ref=gathered_ref.at[:, own],
            send_sem=send_sems.at[step - 1],
            recv_sem=recv_sems.at[step - 1],
            device_id={"seq": peer},
            device_id_type=MESH,
        )
        copy.start()
        copies.append(copy)
    meanwhile()
    for copy in copies:
        copy.wait()


def spread(count_ref, utterance):
    values = jnp.full(utterance.shape, count_ref[0], jnp.int32)
    for u in range(1, count_ref.shape[0]):
        values = jnp.where(utterance == u, count_ref[u], values)
    return values


def lattice_gradients(label_count_ref, frame_count_ref, gathered_ref, labels_ref, prob_ref, hot_ref,
                      logit_ref, table_ref, ahead_ref, back_ref, mass_ref):
    utterances, length = labels_ref.shape
    groups, steps = gathered_ref.shape[:2]
    frames = prob_ref.shape[0] // utterances
    rows = 2 * utterances
    stored = 4 * SPLIT * rows
    slots = length + 1
    width = slots // SPLIT
    pack = utterances // groups
    span = LANES * SPLIT
    shape = (rows, LANES)
    row = lax.broadcasted_iota(jnp.int32, shape, 0)
    lane = lax.broadcasted_iota(jnp.int32, shape, 1)
    forward = row < utterances
    utterance = lax.rem(row, utterances)
    offset = lax.rem(utterance, pack) * slots
    label_rows = table_ref[...]
    label_count = spread(label_count_ref, utterance)
    frame_count = spread(frame_count_ref, utterance)
    first_usable = jnp.where(forward, 0, steps - frame_count)

    label_fill, jump_fill, label_start, blank_start = [], [], [], []
    for r in range(SPLIT):
        run = jnp.where(forward, r, SPLIT - 1 - r)
        j = lane * SPLIT + run
        real = j < length
        label_fill.append(jnp.where(real, 0.0, negative_fill))
        before = jnp.where(forward, j - 1, j + 1)
        here_char = take_lanes(label_rows, jnp.clip(j, 0, LANES - 1))
        before_char = take_lanes(label_rows, jnp.clip(before, 0, LANES - 1))
        can_jump = real & (before >= 0) & (before < length) & (here_char != before_char)
        jump_fill.append(jnp.where(can_jump, 0.0, negative_fill))
        label_begin = j == jnp.where(forward, 0, label_count - 1)
        label_start.append(jnp.where(label_begin, 0.0, negative_fill))
        blank = jnp.where(forward, j, lax.rem(j + 1, span))
        blank_begin = blank == jnp.where(forward, 0, label_count)
        blank_start.append(jnp.where(blank_begin, 0.0, negative_fill))
    blank_index = offset + slots - 1
    inner_of = lax.rem(utterance, pack)
    row_group = utterance // pack

    def frame_row(group, step):
        return jnp.broadcast_to(gathered_ref[group, pl.ds(step, 1), :], shape)

    def raw_emission(step):
        raw = None
        for group in range(groups):
            early = frame_row(group, step)
            late = frame_row(group, steps - 1 - step)
            both = jnp.where(forward, early, late)
            raw = both if raw is None else jnp.where(row_group == group, both, raw)
        return raw

    def label_emissions(raw):
        turned = {}
        for begin in range(0, pack * slots, width):
            turned[begin] = pltpu.roll(raw, LANES - begin, 1) if begin else raw
        found = []
        for r in range(SPLIT):
            chosen = None
            for inner in range(pack):
                ahead = turned[inner * slots + r * width]
                back = turned[inner * slots + (SPLIT - 1 - r) * width]
                both = jnp.where(forward, ahead, back)
                chosen = both if chosen is None else jnp.where(inner_of == inner, both, chosen)
            found.append(chosen + label_fill[r])
        return found

    def behind(values):
        return jnp.where(forward, pltpu.roll(values, 1, 1), pltpu.roll(values, LANES - 1, 1))

    def one_step(step, ahead_slot, back_slot, state, resets):
        labels_v, blanks_v, labels_x, blanks_x = state
        raw = raw_emission(step)
        blank_emission = take_lanes(raw, blank_index)
        label_emission = label_emissions(raw)
        ahead_row = pl.multiple_of(ahead_slot * stored, rows)
        back_row = pl.multiple_of(back_slot * stored, rows)
        full_labels, full_blanks = [], []
        for r in range(SPLIT):
            full_labels.append(labels_v[r] + label_emission[r])
            full_blanks.append(blanks_v[r] + blank_emission)
            ahead_ref[pl.ds(ahead_row + (r) * rows, rows), :] = full_labels[r]
            ahead_ref[pl.ds(ahead_row + (SPLIT + r) * rows, rows), :] = full_blanks[r]
            ahead_ref[pl.ds(ahead_row + (2 * SPLIT + r) * rows, rows), :] = labels_x[r]
            ahead_ref[pl.ds(ahead_row + (3 * SPLIT + r) * rows, rows), :] = blanks_x[r]
            back_ref[pl.ds(back_row + (r) * rows, rows), :] = labels_v[r]
            back_ref[pl.ds(back_row + (SPLIT + r) * rows, rows), :] = blanks_v[r]
            back_ref[pl.ds(back_row + (2 * SPLIT + r) * rows, rows), :] = labels_x[r]
            back_ref[pl.ds(back_row + (3 * SPLIT + r) * rows, rows), :] = blanks_x[r]
        if resets:
            usable = step >= first_usable
        next_labels_v, next_blanks_v, next_labels_x, next_blanks_x = [], [], [], []
        for r in range(SPLIT):
            if r == 0:
                behind_v = behind(full_labels[SPLIT - 1])
                behind_x = behind(labels_x[SPLIT - 1])
            else:
                behind_v = full_labels[r - 1]
                behind_x = labels_x[r - 1]
            jump_v = behind_v + jump_fill[r]
            pivot = jnp.maximum(jnp.maximum(full_blanks[r], full_labels[r]), jump_v)
            fresh_x = (
                jnp.exp2(full_labels[r] - pivot) * labels_x[r]
                + jnp.exp2(full_blanks[r] - pivot) * blanks_x[r]
                + jnp.exp2(jump_v - pivot) * behind_x
            )
            if resets:
                pivot = jnp.where(usable, pivot, label_start[r])
                fresh_x = jnp.where(usable, fresh_x, 1.0)
            next_labels_v.append(pivot)
            next_labels_x.append(fresh_x)
            pivot = jnp.maximum(full_blanks[r], behind_v)
            fresh_x = (
                jnp.exp2(full_blanks[r] - pivot) * blanks_x[r]
                + jnp.exp2(behind_v - pivot) * behind_x
            )
            if resets:
                pivot = jnp.where(usable, pivot, blank_start[r])
                fresh_x = jnp.where(usable, fresh_x, 1.0)
            next_blanks_v.append(pivot)
            next_blanks_x.append(fresh_x)
        return (tuple(next_labels_v), tuple(next_blanks_v), tuple(next_labels_x), tuple(next_blanks_x))

    ones = (jnp.ones(shape, jnp.float32),) * SPLIT

    me = lax.axis_index("seq")
    seq_count = steps // frames

    def history_slot(frame):
        away = lax.rem(frame // frames - me + seq_count, seq_count)
        return (away + seq_count - 1) // seq_count * frames + lax.rem(frame, frames)

    def run_block(resets, block, state):
        for part in range(JOINED):
            state = run_part(resets, block * JOINED + part, state)
        return state

    def run_part(resets, block, state):
        labels_v, blanks_v = state
        full = (labels_v, blanks_v, ones, ones)
        ahead_slot = history_slot(block * UNROLL)
        back_slot = history_slot(steps - (block + 1) * UNROLL)
        for inner in range(UNROLL):
            full = one_step(
                block * UNROLL + inner, ahead_slot + inner, back_slot + UNROLL - 1 - inner, full, resets
            )
        labels_v, blanks_v, labels_x, blanks_x = full
        labels_v = tuple(v + jnp.log2(x) for v, x in zip(labels_v, labels_x))
        blanks_v = tuple(v + jnp.log2(x) for v, x in zip(blanks_v, blanks_x))
        return labels_v, blanks_v

    blocks = steps // (UNROLL * JOINED)
    resetting = (steps // 2) // (UNROLL * JOINED)
    state = (tuple(label_start), tuple(blank_start))
    state = lax.fori_loop(0, resetting, functools.partial(run_block, True), state)
    lax.fori_loop(resetting, blocks, functools.partial(run_block, False), state)

    start = me * frames
    inner_frame = row // utterances

    def posterior_block(block, carry):
        for pair in range(0, 2 * SUBLANES, 2):
            low = block * 2 * SUBLANES + pair
            first = pl.multiple_of(low * stored, rows)

            def ahead(index):
                return jnp.where(
                    forward, ahead_ref[pl.ds(first + index * rows, rows), :],
                    ahead_ref[pl.ds(first + stored + index * rows - utterances, rows), :],
                )

            def back(index):
                return jnp.where(
                    forward, back_ref[pl.ds(first + index * rows + utterances, rows), :],
                    back_ref[pl.ds(first + stored + index * rows, rows), :],
                )

            def term(ahead_index, back_index, turn):
                level, factor = back(back_index), back(2 * SPLIT + back_index)
                if turn:
                    level, factor = pltpu.roll(level, 1, 1), pltpu.roll(factor, 1, 1)
                factor = factor * ahead(2 * SPLIT + ahead_index)
                return (ahead(ahead_index) + level) + jnp.log2(factor)

            terms = [term(r, SPLIT - 1 - r, False) for r in range(SPLIT)]
            terms += [term(SPLIT + r, SPLIT + (SPLIT - r) % SPLIT, r == 0) for r in range(SPLIT)]
            highest = jnp.max(functools.reduce(jnp.maximum, terms), axis=1, keepdims=True)
            powers = [jnp.exp2(value - highest) for value in terms]
            blank_mass = jnp.sum(functools.reduce(jnp.add, powers[SPLIT:]), axis=1, keepdims=True)
            total = blank_mass + jnp.sum(functools.reduce(jnp.add, powers[:SPLIT]), axis=1, keepdims=True)
            usable = start + low + inner_frame < frame_count
            scale = jnp.where(usable, 1.0 / total, 0.0)
            mass = jnp.where(lane == offset + slots - 1, blank_mass, 0.0)
            for inner in range(pack):
                spread_out = None
                for r in range(SPLIT):
                    shift = inner * slots + r * width
                    moved = pltpu.roll(powers[r], shift, 1) if shift else powers[r]
                    spread_out = moved if spread_out is None else spread_out + moved
                mass += spread_out if pack == 1 else jnp.where(inner_of == inner, spread_out, 0.0)
            mass_ref[pl.ds(pl.multiple_of(low * utterances, rows), rows), :] = mass * scale
        return carry

    lax.fori_loop(0, frames // (2 * SUBLANES), posterior_block, 0)

    times = start + lax.broadcasted_iota(jnp.int32, (frames, 1), 0)
    for u in range(utterances):
        own = slice(u * frames, (u + 1) * frames)
        hot = hot_ref[u // pack]
        mass = None
        for part in three_parts(mass_ref[pl.ds(u, frames, stride=utterances), :])[:2]:
            product = jnp.dot(part, hot, preferred_element_type=jnp.float32)
            mass = product if mass is None else mass + product
        kept = jnp.where(times < frame_count_ref[u], prob_ref[own, :] - mass, 0.0)
        logit_ref[own, :] = kept.astype(jnp.bfloat16)
def binary_digits(axis, count):
    index = lax.axis_index(axis)
    digits = []
    step = 1
    while step < count:
        digit = lax.rem(index // step, 2)
        digits.append((axis, digit, index + step * (1 - 2 * digit)))
        step *= 2
    return digits


def link_bits(seq_count, dp_count):
    seq_bits = [("seq", i) for i in range(1, seq_count.bit_length() - 1)]
    dp_bits = [("dp", i) for i in range(dp_count.bit_length() - 1)]
    return seq_bits, dp_bits


def play(orders, sizes, cost):
    free, arrivals, taken = {}, {}, []
    clock = 0.3
    first_left = len(orders)

    def launch(chunk, stage, begin):
        line, rate, latency = cost(orders[chunk][stage])
        end = max(begin, free.get(line, 0.0)) + sizes[chunk] / 2 ** (stage + 1) / rate
        free[line] = end
        arrivals[chunk] = (end + latency, chunk, stage)

    for chunk in range(len(orders)):
        launch(chunk, 0, 0.0)
    while arrivals:
        arrived, chunk, stage = min(arrivals.values())
        del arrivals[chunk]
        clock = max(clock, arrived) + 0.01 + sizes[chunk] / 2 ** (stage + 1) / 4e6
        taken.append((chunk, stage))
        if stage + 1 < len(orders[chunk]):
            launch(chunk, stage + 1, clock)
        if stage == 0:
            first_left -= 1
            if first_left == 0:
                clock += 0.45
    return clock, taken


def transfer_plan(seq_count, dp_count, sizes):
    seq_bits, dp_bits = link_bits(seq_count, dp_count)
    bits = seq_bits + dp_bits
    core = ("seq", 0)

    def cost(bit):
        axis, i = bit
        if bit == core:
            return "core", 0.4e6, 0.9
        far = 2 ** (i - 1) if i else 1
        line = "seq" if axis == "seq" else ("dp first" if i == 0 else "dp rest")
        return line, 0.05e6 / far, 1.0 + 0.7 * far

    if len(bits) <= 4:
        choices = [(core,) + order for order in itertools.permutations(bits)]
    else:
        choices = [(core,) + tuple(bits[k:] + bits[:k]) for k in range(len(bits))]
    orders = [choices[c % len(choices)] for c in range(len(sizes))]
    best = play(orders, sizes, cost)[0]
    for _ in range(4):
        before = best
        for chunk in range(len(sizes)):
            for choice in choices:
                trial = orders[:chunk] + [choice] + orders[chunk + 1:]
                length = play(trial, sizes, cost)[0]
                if length < best:
                    best, orders = length, trial
        if best == before:
            break
    return orders, play(orders, sizes, cost)[1]


def row_chunks(rows):
    quarter = -(-rows // 10 // 8) * 8
    return [(low, min(quarter, rows - low)) for low in range(0, rows, quarter)]


def fused_kernel(seq_count, dp_count, label_count_ref, frame_count_ref, enc_ref, weight_ref,
                 labels_ref, logit_ref, row_ref, out_ref, prob_ref, gathered_ref, hot_ref, table_ref,
                 turned_ref, ahead_ref, back_ref, mass_ref, sent_ref, kept_ref, share_send, share_recv,
                 send_sems, recv_sems, *landed):
    me = lax.axis_index("seq")
    digits = {
        (axis, i): entry
        for axis, count in (("seq", seq_count), ("dp", dp_count))
        for i, entry in enumerate(binary_digits(axis, count))
    }
    greeted = [("seq", lax.rem(me + step, seq_count)) for step in range(1, seq_count)]
    greeted += [(axis, partner) for axis, _, partner in digits.values() if axis == "dp"]
    barrier = pltpu.get_barrier_semaphore()
    for axis, partner in greeted:
        pl.semaphore_signal(barrier, inc=1, device_id={axis: partner}, device_id_type=MESH)

    def before_sending():
        pl.semaphore_wait(barrier, len(greeted))

    def meanwhile():
        turned_ref[...] = jnp.transpose(enc_ref[...])

    share_emissions(seq_count, enc_ref, weight_ref, labels_ref, prob_ref, gathered_ref, hot_ref,
                    table_ref, share_send, share_recv, before_sending, meanwhile)
    lattice_gradients(label_count_ref, frame_count_ref, gathered_ref, labels_ref, prob_ref, hot_ref,
                      logit_ref, table_ref, ahead_ref, back_ref, mass_ref)

    grad = logit_ref[...]
    columns = sent_ref.shape[-1]
    core = digits[("seq", 0)][1]
    even = [grad[:, s * columns:(s + 1) * columns] for s in range(0, seq_count, 2)]
    odd = [grad[:, s * columns:(s + 1) * columns] for s in range(1, seq_count, 2)]

    def fill(target_ref, halves):
        product = jnp.dot(
            turned_ref[...], jnp.concatenate(halves, axis=1), preferred_element_type=jnp.float32
        )
        high = (seq_count // 2).bit_length() - 1
        for h in range(seq_count // 2):
            place = tuple((h >> (high - 1 - i)) & 1 for i in range(high))
            piece = product[:, h * columns:(h + 1) * columns]
            target_ref[place] = piece.reshape(target_ref.shape[high:])

    first = core == 0
    fill(sent_ref, [jnp.where(first, o, e) for e, o in zip(even, odd)])

    seq_bits, dp_bits = link_bits(seq_count, dp_count)
    held = seq_bits[::-1] + dp_bits[::-1]
    rows = out_ref.shape[0]
    chunks = row_chunks(rows)
    stages = len(held) + 1
    orders, taken = transfer_plan(
        seq_count, dp_count, [size * columns * 2 ** stages * 4 for _, size in chunks]
    )
    landing = [landed[c * stages:(c + 1) * stages] for c in range(len(chunks))]
    names = [list(held) for _ in chunks]
    pending = [None] * len(chunks)

    def dense(ref, low, size):
        return ref.at[(slice(None),) * len(held) + (pl.ds(low, size),)]

    def launch(c, stage, source, kept, bit):
        axis, _, partner = digits[bit]
        copy = pltpu.make_async_remote_copy(
            src_ref=source,
            dst_ref=landing[c][stage],
            send_sem=send_sems.at[c],
            recv_sem=recv_sems.at[c, stage],
            device_id={axis: partner},
            device_id_type=MESH,
        )
        copy.start()
        pending[c] = (copy, kept)

    for c, (low, size) in enumerate(chunks):
        launch(c, 0, dense(sent_ref, low, size), dense(kept_ref, low, size), ("seq", 0))
    fill(kept_ref, [jnp.where(first, e, o) for e, o in zip(even, odd)])
    last_first = max(i for i, (_, stage) in enumerate(taken) if stage == 0)
    for i, (c, stage) in enumerate(taken):
        copy, kept = pending[c]
        copy.wait()
        current = landing[c][stage]
        if stage + 1 < stages:
            current[...] += kept[...]
            bit = orders[c][stage + 1]
            ahead = (slice(None),) * names[c].index(bit)
            names[c].remove(bit)
            digit = digits[bit][1]
            launch(c, stage + 1, current.at[ahead + (1 - digit,)], current.at[ahead + (digit,)], bit)
        else:
            low, size = chunks[c]
            out_ref[low:low + size] = (current[...] + kept[...]) / (dp_count * labels_ref.shape[0])
        if i == last_first:
            row_ref[...] = lax.dot_general(
                grad, weight_ref[...], BOTH_LAST, preferred_element_type=jnp.float32
            ).astype(jnp.bfloat16)


def write_results(*refs):
    sems = refs[-1]
    count = (len(refs) - 1) // 2
    copies = [
        pltpu.make_async_copy(refs[i], refs[count + i], sems.at[i]) for i in range(count)
    ]
    for copy in copies:
        copy.start()
    for copy in copies:
        copy.wait()


def shards(enc_rows, out_weight, labels, label_count, frame_count):
    utterances, frames, width = enc_rows.shape
    vocabulary = out_weight.shape[1]
    length = labels.shape[1]
    slots = length + 1
    pack = LANES // slots
    groups = utterances // pack
    seq_count = lax.axis_size("seq")
    flat_rows = enc_rows.reshape(utterances * frames, width)
    vmem = pl.BlockSpec(memory_space=pltpu.VMEM)

    rows = 2 * utterances
    steps = seq_count * frames
    dp_count = lax.axis_size("dp")
    held = sum(link_bits(seq_count, dp_count), [])
    block_rows, block_columns = width // dp_count, vocabulary // seq_count
    whole_block = (2,) * len(held) + (block_rows, block_columns)
    chunks = row_chunks(block_rows)
    landed = [
        pltpu.VMEM((2,) * (len(held) - stage) + (size, block_columns), jnp.float32)
        for low, size in chunks
        for stage in range(len(held) + 1)
    ]
    smem = pl.BlockSpec(memory_space=pltpu.SMEM)
    logit_grad, row_grad, weight_grad = pl.pallas_call(
        functools.partial(fused_kernel, seq_count, dp_count),
        out_shape=(
            pltpu.VMEM((utterances * frames, vocabulary), jnp.bfloat16),
            pltpu.VMEM((utterances * frames, width), jnp.bfloat16),
            pltpu.VMEM((block_rows, block_columns), jnp.float32),
        ),
        in_specs=[smem, smem] + [vmem] * 3,
        out_specs=(vmem, vmem, vmem),
        scratch_shapes=[
            pltpu.VMEM((utterances * frames, vocabulary), jnp.float32),
            pltpu.VMEM((groups, steps, LANES), jnp.float32),
            pltpu.VMEM((groups, LANES, vocabulary), jnp.bfloat16),
            pltpu.VMEM((rows, LANES), jnp.int32),
            pltpu.VMEM((width, utterances * frames), jnp.bfloat16),
            pltpu.VMEM((2 * frames * 4 * SPLIT * rows, LANES), jnp.float32),
            pltpu.VMEM((2 * frames * 4 * SPLIT * rows, LANES), jnp.float32),
            pltpu.VMEM((utterances * frames, LANES), jnp.float32),
            pltpu.VMEM(whole_block, jnp.float32),
            pltpu.VMEM(whole_block, jnp.float32),
            pltpu.SemaphoreType.DMA((seq_count - 1,)),
            pltpu.SemaphoreType.DMA((seq_count - 1,)),
            pltpu.SemaphoreType.DMA((len(chunks),)),
            pltpu.SemaphoreType.DMA((len(chunks), len(held) + 1)),
        ] + landed,
        compiler_params=pltpu.CompilerParams(
            collective_id=0, has_side_effects=True, vmem_limit_bytes=60 * 1024 * 1024
        ),
        name="fused",
    )(label_count, frame_count, flat_rows, out_weight, labels)
    logit_grad, row_grad, weight_grad = pl.pallas_call(
        write_results,
        out_shape=(
            jax.ShapeDtypeStruct((utterances * frames, vocabulary), jnp.bfloat16),
            jax.ShapeDtypeStruct((utterances * frames, width), jnp.bfloat16),
            jax.ShapeDtypeStruct((block_rows, block_columns), jnp.float32),
        ),
        in_specs=[vmem] * 3,
        out_specs=(pl.BlockSpec(memory_space=pl.ANY),) * 3,
        scratch_shapes=[pltpu.SemaphoreType.DMA((3,))],
        compiler_params=pltpu.CompilerParams(vmem_limit_bytes=4 * 1024 * 1024),
        name="write_results",
    )(logit_grad, row_grad, weight_grad)
    return (
        logit_grad.reshape(utterances, frames, vocabulary),
        row_grad.reshape(utterances, frames, width),
        weight_grad,
    )


def solution(mesh):
    placed = (P("dp", "seq", None), P(), P("dp", None), P("dp"), P("dp"))
    return jax.shard_map(
        shards,
        mesh=mesh,
        in_specs=placed,
        out_specs=(P("dp", "seq", None), P("dp", "seq", None), P("dp", "seq")),
        check_vma=False,
    )
```

```python
import functools
import itertools

import jax
import jax.numpy as jnp
from jax import lax
from jax.experimental import pallas as pl
from jax.experimental.pallas import tpu as pltpu
from jax.sharding import PartitionSpec as P

negative_fill = -1e30
LOG2_E = 1.4426950408889634
LANES = 128
SUBLANES = 8
SPLIT = 4
UNROLL = 32
JOINED = 2
MESH = pl.DeviceIdType.MESH
BOTH_LAST = (((1,), (1,)), ((), ()))


def three_parts(values):
    high = values.astype(jnp.bfloat16)
    rest = values - high.astype(jnp.float32)
    middle = rest.astype(jnp.bfloat16)
    low = (rest - middle.astype(jnp.float32)).astype(jnp.bfloat16)
    return high, middle, low


def label_table(labels_ref, table_ref):
    utterances, length = labels_ref.shape
    table_ref[...] = jnp.zeros_like(table_ref)
    table_ref[0:utterances, 0:length] = labels_ref[...]
    table_ref[utterances:2 * utterances, 0:length] = labels_ref[...]
    return table_ref[...]


def take_lanes(values, index):
    return jnp.take_along_axis(values, index, axis=1)


def character_tables(labels_ref, table_ref, hot_ref):
    groups, _, vocabulary = hot_ref.shape
    utterances, length = labels_ref.shape
    slots = length + 1
    pack = utterances // groups
    width = slots // SPLIT
    table = label_table(labels_ref, table_ref)
    lane = lax.broadcasted_iota(jnp.int32, table.shape, 1)
    within = lax.rem(lane, slots)
    order = lax.rem(within, width) * SPLIT + within // width
    chars = take_lanes(table, order).astype(jnp.float32)
    row_lane = lax.broadcasted_iota(jnp.int32, (1, LANES), 1)
    columns = lax.broadcasted_iota(jnp.int32, (LANES, LANES), 1).astype(jnp.float32)
    for group in range(groups):
        first = group * pack
        line = chars[first:first + 1, :]
        for inner in range(1, pack):
            line = jnp.where(row_lane >= inner * slots, chars[first + inner:first + inner + 1, :], line)
        down = jnp.transpose(jnp.broadcast_to(line, (LANES, LANES)))
        for low in range(0, vocabulary, LANES):
            hot_ref[group, :, low:low + LANES] = jnp.where(
                down == columns + float(low), 1.0, 0.0
            ).astype(jnp.bfloat16)


def share_emissions(seq_count, enc_ref, weight_ref, labels_ref, prob_ref, gathered_ref, hot_ref,
                    table_ref, send_sems, recv_sems, before_sending, meanwhile, loads):
    utterances, length = labels_ref.shape
    me = lax.axis_index("seq")
    frames = enc_ref.shape[0] // utterances
    groups = gathered_ref.shape[0]
    pack = utterances // groups
    slots = length + 1
    own = pl.ds(pl.multiple_of(me * frames, frames), frames)
    character_tables(labels_ref, table_ref, hot_ref)
    logits = None
    half = weight_ref.shape[0] // 2
    for part, pair in enumerate(loads):
        for load in pair:
            load.wait()
        run = slice(part * half, (part + 1) * half)
        product = jnp.dot(enc_ref[:, run], weight_ref[run, :], preferred_element_type=jnp.float32)
        logits = product if logits is None else logits + product
    highest = jnp.max(logits, axis=1, keepdims=True)
    shifted = logits - highest
    powers = jnp.exp(shifted)
    total = jnp.sum(powers, axis=1, keepdims=True)
    logprob = shifted - jnp.log(total)
    prob_ref[...] = powers * (1.0 / total)
    lane = lax.broadcasted_iota(jnp.int32, (frames, LANES), 1)
    for group in range(groups):
        rows = pack * frames
        mine = logprob[group * rows:(group + 1) * rows]
        picked = None
        for part in three_parts(mine):
            product = lax.dot_general(part, hot_ref[group], BOTH_LAST, preferred_element_type=jnp.float32)
            picked = product if picked is None else picked + product
        packed = picked[:frames]
        for inner in range(1, pack):
            packed = jnp.where(lane >= inner * slots, picked[inner * frames:(inner + 1) * frames], packed)
        gathered_ref[group, own, :] = packed * LOG2_E
    before_sending()
    copies = []
    for step in range(1, seq_count):
        peer = lax.rem(me + step, seq_count)
        copy = pltpu.make_async_remote_copy(
            src_ref=gathered_ref.at[:, own],
            dst_ref=gathered_ref.at[:, own],
            send_sem=send_sems.at[step - 1],
            recv_sem=recv_sems.at[step - 1],
            device_id={"seq": peer},
            device_id_type=MESH,
        )
        copy.start()
        copies.append(copy)
    meanwhile()
    for copy in copies:
        copy.wait()


def spread(count_ref, utterance):
    values = jnp.full(utterance.shape, count_ref[0], jnp.int32)
    for u in range(1, count_ref.shape[0]):
        values = jnp.where(utterance == u, count_ref[u], values)
    return values


def lattice_gradients(label_count_ref, frame_count_ref, gathered_ref, labels_ref, prob_ref, hot_ref,
                      logit_ref, table_ref, ahead_ref, back_ref, mass_ref):
    utterances, length = labels_ref.shape
    groups, steps = gathered_ref.shape[:2]
    frames = prob_ref.shape[0] // utterances
    rows = 2 * utterances
    stored = 4 * SPLIT * rows
    slots = length + 1
    width = slots // SPLIT
    pack = utterances // groups
    span = LANES * SPLIT
    shape = (rows, LANES)
    row = lax.broadcasted_iota(jnp.int32, shape, 0)
    lane = lax.broadcasted_iota(jnp.int32, shape, 1)
    forward = row < utterances
    utterance = lax.rem(row, utterances)
    offset = lax.rem(utterance, pack) * slots
    label_rows = table_ref[...]
    label_count = spread(label_count_ref, utterance)
    frame_count = spread(frame_count_ref, utterance)
    first_usable = jnp.where(forward, 0, steps - frame_count)

    label_fill, jump_fill, label_start, blank_start = [], [], [], []
    for r in range(SPLIT):
        run = jnp.where(forward, r, SPLIT - 1 - r)
        j = lane * SPLIT + run
        real = j < length
        label_fill.append(jnp.where(real, 0.0, negative_fill))
        before = jnp.where(forward, j - 1, j + 1)
        here_char = take_lanes(label_rows, jnp.clip(j, 0, LANES - 1))
        before_char = take_lanes(label_rows, jnp.clip(before, 0, LANES - 1))
        can_jump = real & (before >= 0) & (before < length) & (here_char != before_char)
        jump_fill.append(jnp.where(can_jump, 0.0, negative_fill))
        label_begin = j == jnp.where(forward, 0, label_count - 1)
        label_start.append(jnp.where(label_begin, 0.0, negative_fill))
        blank = jnp.where(forward, j, lax.rem(j + 1, span))
        blank_begin = blank == jnp.where(forward, 0, label_count)
        blank_start.append(jnp.where(blank_begin, 0.0, negative_fill))
    blank_index = offset + slots - 1
    inner_of = lax.rem(utterance, pack)
    row_group = utterance // pack

    def frame_row(group, step):
        return jnp.broadcast_to(gathered_ref[group, pl.ds(step, 1), :], shape)

    def raw_emission(step):
        raw = None
        for group in range(groups):
            early = frame_row(group, step)
            late = frame_row(group, steps - 1 - step)
            both = jnp.where(forward, early, late)
            raw = both if raw is None else jnp.where(row_group == group, both, raw)
        return raw

    def label_emissions(raw):
        turned = {}
        for begin in range(0, pack * slots, width):
            turned[begin] = pltpu.roll(raw, LANES - begin, 1) if begin else raw
        found = []
        for r in range(SPLIT):
            chosen = None
            for inner in range(pack):
                ahead = turned[inner * slots + r * width]
                back = turned[inner * slots + (SPLIT - 1 - r) * width]
                both = jnp.where(forward, ahead, back)
                chosen = both if chosen is None else jnp.where(inner_of == inner, both, chosen)
            found.append(chosen + label_fill[r])
        return found

    def behind(values):
        return jnp.where(forward, pltpu.roll(values, 1, 1), pltpu.roll(values, LANES - 1, 1))

    def one_step(step, ahead_slot, back_slot, state, resets):
        labels_v, blanks_v, labels_x, blanks_x = state
        raw = raw_emission(step)
        blank_emission = take_lanes(raw, blank_index)
        label_emission = label_emissions(raw)
        ahead_row = pl.multiple_of(ahead_slot * stored, rows)
        back_row = pl.multiple_of(back_slot * stored, rows)
        full_labels, full_blanks = [], []
        for r in range(SPLIT):
            full_labels.append(labels_v[r] + label_emission[r])
            full_blanks.append(blanks_v[r] + blank_emission)
            ahead_ref[pl.ds(ahead_row + (r) * rows, rows), :] = full_labels[r]
            ahead_ref[pl.ds(ahead_row + (SPLIT + r) * rows, rows), :] = full_blanks[r]
            ahead_ref[pl.ds(ahead_row + (2 * SPLIT + r) * rows, rows), :] = labels_x[r]
            ahead_ref[pl.ds(ahead_row + (3 * SPLIT + r) * rows, rows), :] = blanks_x[r]
            back_ref[pl.ds(back_row + (r) * rows, rows), :] = labels_v[r]
            back_ref[pl.ds(back_row + (SPLIT + r) * rows, rows), :] = blanks_v[r]
            back_ref[pl.ds(back_row + (2 * SPLIT + r) * rows, rows), :] = labels_x[r]
            back_ref[pl.ds(back_row + (3 * SPLIT + r) * rows, rows), :] = blanks_x[r]
        if resets:
            usable = step >= first_usable
        next_labels_v, next_blanks_v, next_labels_x, next_blanks_x = [], [], [], []
        for r in range(SPLIT):
            if r == 0:
                behind_v = behind(full_labels[SPLIT - 1])
                behind_x = behind(labels_x[SPLIT - 1])
            else:
                behind_v = full_labels[r - 1]
                behind_x = labels_x[r - 1]
            jump_v = behind_v + jump_fill[r]
            pivot = jnp.maximum(jnp.maximum(full_blanks[r], full_labels[r]), jump_v)
            fresh_x = (
                jnp.exp2(full_labels[r] - pivot) * labels_x[r]
                + jnp.exp2(full_blanks[r] - pivot) * blanks_x[r]
                + jnp.exp2(jump_v - pivot) * behind_x
            )
            if resets:
                pivot = jnp.where(usable, pivot, label_start[r])
                fresh_x = jnp.where(usable, fresh_x, 1.0)
            next_labels_v.append(pivot)
            next_labels_x.append(fresh_x)
            pivot = jnp.maximum(full_blanks[r], behind_v)
            fresh_x = (
                jnp.exp2(full_blanks[r] - pivot) * blanks_x[r]
                + jnp.exp2(behind_v - pivot) * behind_x
            )
            if resets:
                pivot = jnp.where(usable, pivot, blank_start[r])
                fresh_x = jnp.where(usable, fresh_x, 1.0)
            next_blanks_v.append(pivot)
            next_blanks_x.append(fresh_x)
        return (tuple(next_labels_v), tuple(next_blanks_v), tuple(next_labels_x), tuple(next_blanks_x))

    ones = (jnp.ones(shape, jnp.float32),) * SPLIT

    me = lax.axis_index("seq")
    seq_count = steps // frames

    def history_slot(frame):
        away = lax.rem(frame // frames - me + seq_count, seq_count)
        return (away + seq_count - 1) // seq_count * frames + lax.rem(frame, frames)

    def run_block(resets, block, state):
        for part in range(JOINED):
            state = run_part(resets, block * JOINED + part, state)
        return state

    def run_part(resets, block, state):
        labels_v, blanks_v = state
        full = (labels_v, blanks_v, ones, ones)
        ahead_slot = history_slot(block * UNROLL)
        back_slot = history_slot(steps - (block + 1) * UNROLL)
        for inner in range(UNROLL):
            full = one_step(
                block * UNROLL + inner, ahead_slot + inner, back_slot + UNROLL - 1 - inner, full, resets
            )
        labels_v, blanks_v, labels_x, blanks_x = full
        labels_v = tuple(v + jnp.log2(x) for v, x in zip(labels_v, labels_x))
        blanks_v = tuple(v + jnp.log2(x) for v, x in zip(blanks_v, blanks_x))
        return labels_v, blanks_v

    blocks = steps // (UNROLL * JOINED)
    resetting = (steps // 2) // (UNROLL * JOINED)
    state = (tuple(label_start), tuple(blank_start))
    state = lax.fori_loop(0, resetting, functools.partial(run_block, True), state)
    lax.fori_loop(resetting, blocks, functools.partial(run_block, False), state)

    start = me * frames
    inner_frame = row // utterances

    def posterior_block(block, carry):
        for pair in range(0, 2 * SUBLANES, 2):
            low = block * 2 * SUBLANES + pair
            first = pl.multiple_of(low * stored, rows)

            def ahead(index):
                return jnp.where(
                    forward, ahead_ref[pl.ds(first + index * rows, rows), :],
                    ahead_ref[pl.ds(first + stored + index * rows - utterances, rows), :],
                )

            def back(index):
                return jnp.where(
                    forward, back_ref[pl.ds(first + index * rows + utterances, rows), :],
                    back_ref[pl.ds(first + stored + index * rows, rows), :],
                )

            def term(ahead_index, back_index, turn):
                level, factor = back(back_index), back(2 * SPLIT + back_index)
                if turn:
                    level, factor = pltpu.roll(level, 1, 1), pltpu.roll(factor, 1, 1)
                factor = factor * ahead(2 * SPLIT + ahead_index)
                return (ahead(ahead_index) + level) + jnp.log2(factor)

            terms = [term(r, SPLIT - 1 - r, False) for r in range(SPLIT)]
            terms += [term(SPLIT + r, SPLIT + (SPLIT - r) % SPLIT, r == 0) for r in range(SPLIT)]
            highest = jnp.max(functools.reduce(jnp.maximum, terms), axis=1, keepdims=True)
            powers = [jnp.exp2(value - highest) for value in terms]
            blank_mass = jnp.sum(functools.reduce(jnp.add, powers[SPLIT:]), axis=1, keepdims=True)
            total = blank_mass + jnp.sum(functools.reduce(jnp.add, powers[:SPLIT]), axis=1, keepdims=True)
            usable = start + low + inner_frame < frame_count
            scale = jnp.where(usable, 1.0 / total, 0.0)
            mass = jnp.where(lane == offset + slots - 1, blank_mass, 0.0)
            for inner in range(pack):
                spread_out = None
                for r in range(SPLIT):
                    shift = inner * slots + r * width
                    moved = pltpu.roll(powers[r], shift, 1) if shift else powers[r]
                    spread_out = moved if spread_out is None else spread_out + moved
                mass += spread_out if pack == 1 else jnp.where(inner_of == inner, spread_out, 0.0)
            mass_ref[pl.ds(pl.multiple_of(low * utterances, rows), rows), :] = mass * scale
        return carry

    lax.fori_loop(0, frames // (2 * SUBLANES), posterior_block, 0)

    times = start + lax.broadcasted_iota(jnp.int32, (frames, 1), 0)
    for u in range(utterances):
        own = slice(u * frames, (u + 1) * frames)
        hot = hot_ref[u // pack]
        mass = None
        for part in three_parts(mass_ref[pl.ds(u, frames, stride=utterances), :])[:2]:
            product = jnp.dot(part, hot, preferred_element_type=jnp.float32)
            mass = product if mass is None else mass + product
        kept = jnp.where(times < frame_count_ref[u], prob_ref[own, :] - mass, 0.0)
        logit_ref[own, :] = kept.astype(jnp.bfloat16)
def binary_digits(axis, count):
    index = lax.axis_index(axis)
    digits = []
    step = 1
    while step < count:
        digit = lax.rem(index // step, 2)
        digits.append((axis, digit, index + step * (1 - 2 * digit)))
        step *= 2
    return digits


def link_bits(seq_count, dp_count):
    seq_bits = [("seq", i) for i in range(1, seq_count.bit_length() - 1)]
    dp_bits = [("dp", i) for i in range(dp_count.bit_length() - 1)]
    return seq_bits, dp_bits


def play(orders, sizes, cost):
    free, arrivals, taken = {}, {}, []
    clock = 0.3
    first_left = len(orders)

    def launch(chunk, stage, begin):
        line, rate, latency = cost(orders[chunk][stage])
        end = max(begin, free.get(line, 0.0)) + sizes[chunk] / 2 ** (stage + 1) / rate
        free[line] = end
        arrivals[chunk] = (end + latency, chunk, stage)

    for chunk in range(len(orders)):
        launch(chunk, 0, 0.0)
    while arrivals:
        arrived, chunk, stage = min(arrivals.values())
        del arrivals[chunk]
        clock = max(clock, arrived) + 0.01 + sizes[chunk] / 2 ** (stage + 1) / 4e6
        taken.append((chunk, stage))
        if stage + 1 < len(orders[chunk]):
            launch(chunk, stage + 1, clock)
        if stage == 0:
            first_left -= 1
            if first_left == 0:
                clock += 0.45
    return clock, taken


def transfer_plan(seq_count, dp_count, sizes):
    seq_bits, dp_bits = link_bits(seq_count, dp_count)
    bits = seq_bits + dp_bits
    core = ("seq", 0)

    def cost(bit):
        axis, i = bit
        if bit == core:
            return "core", 0.4e6, 0.9
        far = 2 ** (i - 1) if i else 1
        line = "seq" if axis == "seq" else ("dp first" if i == 0 else "dp rest")
        return line, 0.05e6 / far, 1.0 + 0.7 * far

    if len(bits) <= 4:
        choices = [(core,) + order for order in itertools.permutations(bits)]
    else:
        choices = [(core,) + tuple(bits[k:] + bits[:k]) for k in range(len(bits))]
    orders = [choices[c % len(choices)] for c in range(len(sizes))]
    best = play(orders, sizes, cost)[0]
    for _ in range(4):
        before = best
        for chunk in range(len(sizes)):
            for choice in choices:
                trial = orders[:chunk] + [choice] + orders[chunk + 1:]
                length = play(trial, sizes, cost)[0]
                if length < best:
                    best, orders = length, trial
        if best == before:
            break
    return orders, play(orders, sizes, cost)[1]


def row_chunks(rows):
    quarter = -(-rows // 10 // 8) * 8
    return [(low, min(quarter, rows - low)) for low in range(0, rows, quarter)]


def fused_kernel(seq_count, dp_count, label_count_ref, frame_count_ref, enc_input, weight_input,
                 labels_ref, logit_ref, row_ref, out_ref, prob_ref, gathered_ref, hot_ref, table_ref,
                 turned_ref, ahead_ref, back_ref, mass_ref, sent_ref, kept_ref, share_send, share_recv,
                 send_sems, recv_sems, enc_ref, weight_ref, load_sems, *landed):
    half = weight_ref.shape[0] // 2
    loads = []
    for part in range(2):
        run = pl.ds(part * half, half)
        loads.append((
            pltpu.make_async_copy(weight_input.at[run], weight_ref.at[run], load_sems.at[part, 0]),
            pltpu.make_async_copy(enc_input.at[:, run], enc_ref.at[:, run], load_sems.at[part, 1]),
        ))
        for load in loads[-1]:
            load.start()
    me = lax.axis_index("seq")
    digits = {
        (axis, i): entry
        for axis, count in (("seq", seq_count), ("dp", dp_count))
        for i, entry in enumerate(binary_digits(axis, count))
    }
    greeted = [("seq", lax.rem(me + step, seq_count)) for step in range(1, seq_count)]
    greeted += [(axis, partner) for axis, _, partner in digits.values() if axis == "dp"]
    barrier = pltpu.get_barrier_semaphore()
    for axis, partner in greeted:
        pl.semaphore_signal(barrier, inc=1, device_id={axis: partner}, device_id_type=MESH)

    def before_sending():
        pl.semaphore_wait(barrier, len(greeted))

    def meanwhile():
        turned_ref[...] = jnp.transpose(enc_ref[...])

    share_emissions(seq_count, enc_ref, weight_ref, labels_ref, prob_ref, gathered_ref, hot_ref,
                    table_ref, share_send, share_recv, before_sending, meanwhile, loads)
    lattice_gradients(label_count_ref, frame_count_ref, gathered_ref, labels_ref, prob_ref, hot_ref,
                      logit_ref, table_ref, ahead_ref, back_ref, mass_ref)

    grad = logit_ref[...]
    columns = sent_ref.shape[-1]
    core = digits[("seq", 0)][1]
    even = [grad[:, s * columns:(s + 1) * columns] for s in range(0, seq_count, 2)]
    odd = [grad[:, s * columns:(s + 1) * columns] for s in range(1, seq_count, 2)]

    def fill(target_ref, halves):
        product = jnp.dot(
            turned_ref[...], jnp.concatenate(halves, axis=1), preferred_element_type=jnp.float32
        )
        high = (seq_count // 2).bit_length() - 1
        for h in range(seq_count // 2):
            place = tuple((h >> (high - 1 - i)) & 1 for i in range(high))
            piece = product[:, h * columns:(h + 1) * columns]
            target_ref[place] = piece.reshape(target_ref.shape[high:])

    first = core == 0
    fill(sent_ref, [jnp.where(first, o, e) for e, o in zip(even, odd)])

    seq_bits, dp_bits = link_bits(seq_count, dp_count)
    held = seq_bits[::-1] + dp_bits[::-1]
    rows = out_ref.shape[0]
    chunks = row_chunks(rows)
    stages = len(held) + 1
    orders, taken = transfer_plan(
        seq_count, dp_count, [size * columns * 2 ** stages * 4 for _, size in chunks]
    )
    landing = [landed[c * stages:(c + 1) * stages] for c in range(len(chunks))]
    names = [list(held) for _ in chunks]
    pending = [None] * len(chunks)

    def dense(ref, low, size):
        return ref.at[(slice(None),) * len(held) + (pl.ds(low, size),)]

    def launch(c, stage, source, kept, bit):
        axis, _, partner = digits[bit]
        copy = pltpu.make_async_remote_copy(
            src_ref=source,
            dst_ref=landing[c][stage],
            send_sem=send_sems.at[c],
            recv_sem=recv_sems.at[c, stage],
            device_id={axis: partner},
            device_id_type=MESH,
        )
        copy.start()
        pending[c] = (copy, kept)

    for c, (low, size) in enumerate(chunks):
        launch(c, 0, dense(sent_ref, low, size), dense(kept_ref, low, size), ("seq", 0))
    fill(kept_ref, [jnp.where(first, e, o) for e, o in zip(even, odd)])
    last_first = max(i for i, (_, stage) in enumerate(taken) if stage == 0)
    for i, (c, stage) in enumerate(taken):
        copy, kept = pending[c]
        copy.wait()
        current = landing[c][stage]
        if stage + 1 < stages:
            current[...] += kept[...]
            bit = orders[c][stage + 1]
            ahead = (slice(None),) * names[c].index(bit)
            names[c].remove(bit)
            digit = digits[bit][1]
            launch(c, stage + 1, current.at[ahead + (1 - digit,)], current.at[ahead + (digit,)], bit)
        else:
            low, size = chunks[c]
            out_ref[low:low + size] = (current[...] + kept[...]) / (dp_count * labels_ref.shape[0])
        if i == last_first:
            row_ref[...] = lax.dot_general(
                grad, weight_ref[...], BOTH_LAST, preferred_element_type=jnp.float32
            ).astype(jnp.bfloat16)


def write_results(*refs):
    sems = refs[-1]
    count = (len(refs) - 1) // 2
    copies = [
        pltpu.make_async_copy(refs[i], refs[count + i], sems.at[i]) for i in range(count)
    ]
    for copy in copies:
        copy.start()
    for copy in copies:
        copy.wait()


def shards(enc_rows, out_weight, labels, label_count, frame_count):
    utterances, frames, width = enc_rows.shape
    vocabulary = out_weight.shape[1]
    length = labels.shape[1]
    slots = length + 1
    pack = LANES // slots
    groups = utterances // pack
    seq_count = lax.axis_size("seq")
    flat_rows = enc_rows.reshape(utterances * frames, width)
    vmem = pl.BlockSpec(memory_space=pltpu.VMEM)

    rows = 2 * utterances
    steps = seq_count * frames
    dp_count = lax.axis_size("dp")
    held = sum(link_bits(seq_count, dp_count), [])
    block_rows, block_columns = width // dp_count, vocabulary // seq_count
    whole_block = (2,) * len(held) + (block_rows, block_columns)
    chunks = row_chunks(block_rows)
    landed = [
        pltpu.VMEM((2,) * (len(held) - stage) + (size, block_columns), jnp.float32)
        for low, size in chunks
        for stage in range(len(held) + 1)
    ]
    smem = pl.BlockSpec(memory_space=pltpu.SMEM)
    logit_grad, row_grad, weight_grad = pl.pallas_call(
        functools.partial(fused_kernel, seq_count, dp_count),
        out_shape=(
            pltpu.VMEM((utterances * frames, vocabulary), jnp.bfloat16),
            pltpu.VMEM((utterances * frames, width), jnp.bfloat16),
            pltpu.VMEM((block_rows, block_columns), jnp.float32),
        ),
        in_specs=[smem, smem] + [pl.BlockSpec(memory_space=pltpu.HBM)] * 2 + [vmem],
        out_specs=(vmem, vmem, vmem),
        scratch_shapes=[
            pltpu.VMEM((utterances * frames, vocabulary), jnp.float32),
            pltpu.VMEM((groups, steps, LANES), jnp.float32),
            pltpu.VMEM((groups, LANES, vocabulary), jnp.bfloat16),
            pltpu.VMEM((rows, LANES), jnp.int32),
            pltpu.VMEM((width, utterances * frames), jnp.bfloat16),
            pltpu.VMEM((2 * frames * 4 * SPLIT * rows, LANES), jnp.float32),
            pltpu.VMEM((2 * frames * 4 * SPLIT * rows, LANES), jnp.float32),
            pltpu.VMEM((utterances * frames, LANES), jnp.float32),
            pltpu.VMEM(whole_block, jnp.float32),
            pltpu.VMEM(whole_block, jnp.float32),
            pltpu.SemaphoreType.DMA((seq_count - 1,)),
            pltpu.SemaphoreType.DMA((seq_count - 1,)),
            pltpu.SemaphoreType.DMA((len(chunks),)),
            pltpu.SemaphoreType.DMA((len(chunks), len(held) + 1)),
            pltpu.VMEM(flat_rows.shape, flat_rows.dtype),
            pltpu.VMEM(out_weight.shape, out_weight.dtype),
            pltpu.SemaphoreType.DMA((2, 2)),
        ] + landed,
        compiler_params=pltpu.CompilerParams(
            collective_id=0, has_side_effects=True, vmem_limit_bytes=60 * 1024 * 1024
        ),
        name="fused",
    )(label_count, frame_count, flat_rows, out_weight, labels)
    logit_grad, row_grad, weight_grad = pl.pallas_call(
        write_results,
        out_shape=(
            jax.ShapeDtypeStruct((utterances * frames, vocabulary), jnp.bfloat16),
            jax.ShapeDtypeStruct((utterances * frames, width), jnp.bfloat16),
            jax.ShapeDtypeStruct((block_rows, block_columns), jnp.float32),
        ),
        in_specs=[vmem] * 3,
        out_specs=(pl.BlockSpec(memory_space=pl.ANY),) * 3,
        scratch_shapes=[pltpu.SemaphoreType.DMA((3,))],
        compiler_params=pltpu.CompilerParams(vmem_limit_bytes=4 * 1024 * 1024),
        name="write_results",
    )(logit_grad, row_grad, weight_grad)
    return (
        logit_grad.reshape(utterances, frames, vocabulary),
        row_grad.reshape(utterances, frames, width),
        weight_grad,
    )


def solution(mesh):
    placed = (P("dp", "seq", None), P(), P("dp", None), P("dp"), P("dp"))
    return jax.shard_map(
        shards,
        mesh=mesh,
        in_specs=placed,
        out_specs=(P("dp", "seq", None), P("dp", "seq", None), P("dp", "seq")),
        check_vma=False,
    )
```
